32 devices in a mesh: tm: 2 (over x), row: 4 (over z), col: 4 (over y, core).
Axes of the slice: x: 2, y: 2, z: 4, core: 2. Of those that a mesh axis runs over, the one named last changes fastest.
Arguments:
- features: bfloat16 [4, 60, 104, 128], P('tm', 'row', 'col'), may hold values from -13 to 13
- cotangent: bfloat16 [4, 60, 104, 128], P('tm', 'row', 'col'), may hold values from -7 to 7
- conv_one: bfloat16 [27, 128, 128], replicated, may hold values from -0.109375 to 0.109375
- conv_two: bfloat16 [27, 128, 128], replicated, may hold values from -0.109375 to 0.109375
- gain_one: float32 [128], replicated, may hold values from 0.25 to 1.75
- shift_one: float32 [128], replicated, may hold values from -0.6 to 0.6
- gain_two: float32 [128], replicated, may hold values from 0.25 to 1.75
- shift_two: float32 [128], replicated, may hold values from -0.6 to 0.6
Outputs:
- block_out: bfloat16 [4, 60, 104, 128], P('tm', 'row', 'col')
- grad_input: bfloat16 [4, 60, 104, 128], P('tm', 'row', 'col')
- grad_conv_one: float32 [27, 128, 128], replicated
- grad_conv_two: float32 [27, 128, 128], replicated
The draws below stay inside these ranges and needn't reach their ends.
All inputs are finite; a program needn't handle non-finite values.
Results may differ from the reference program's by a relative error of at most 0.0034.
Values may be sent and summed in bfloat16 or wider, within the bound.
A program may use at most 128 MiB of HBM per device.

```python
import jax
import jax.numpy as jnp
from jax import lax

C = 128
GROUPS = 32
TAPS = 27
FRAMES = 4
HEIGHT = 60
WIDTH = 104


def spatial_ramps():
    frame_pos = jnp.arange(FRAMES, dtype=jnp.float32) / max(FRAMES - 1, 1)
    row_pos = jnp.arange(HEIGHT, dtype=jnp.float32) / max(HEIGHT - 1, 1)
    col_pos = jnp.arange(WIDTH, dtype=jnp.float32) / max(WIDTH - 1, 1)
    return (frame_pos, row_pos, col_pos)


def draw_features(key, part):
    key_base, key_offset = jax.random.split(jax.random.fold_in(key, 11), 2)
    shape_full = (FRAMES, HEIGHT, WIDTH, C)
    frame_pos, row_pos, col_pos = spatial_ramps()
    frame_factor = 1.0 + 2.0 * frame_pos
    row_factor = 0.4 + 0.6 * row_pos
    col_factor = 1.0 - 0.6 * col_pos
    factor = frame_factor[:, None, None] * row_factor[None, :, None] * col_factor[None, None, :]
    place_offset = 0.5 * (col_pos[None, :] - row_pos[:, None])
    offset = 0.5 * jax.random.uniform(key_offset, (C,), jnp.float32, -1.0, 1.0)
    base = jnp.clip(jax.random.normal(key_base, shape_full, jnp.float32), -4.0, 4.0)
    values = base * factor[:, :, :, None] + place_offset[None, :, :, None] + offset
    return values.astype(jnp.bfloat16)


def draw_cotangent(key, part):
    key_noise, key_offset = jax.random.split(jax.random.fold_in(key, 23), 2)
    shape_full = (FRAMES, HEIGHT, WIDTH, C)
    frame_pos, row_pos, col_pos = spatial_ramps()
    reach = 0.25 + 0.5 * (frame_pos[:, None, None] + row_pos[None, :, None] + col_pos[None, None, :])
    offset = jax.random.uniform(key_offset, (C,), jnp.float32, -1.0, 1.0)
    noise = jnp.clip(jax.random.normal(key_noise, shape_full, jnp.float32), -5.0, 5.0)
    values = noise + reach[:, :, :, None] * offset
    return values.astype(jnp.bfloat16)


def centred(own_key, dims, scale, most, held_as=jnp.bfloat16):
    result = jax.random.normal(own_key, dims, jnp.float32) * scale
    return jnp.minimum(jnp.maximum(result, -most), most).astype(held_as)


def setup_inputs(seed: int = 0) -> dict:
    splits = jax.random.split(jax.random.key(seed), 9)
    features = draw_features(jax.random.fold_in(splits[8], 71), 0)
    cotangent = draw_cotangent(jax.random.fold_in(splits[8], 71), 0)
    conv_one = centred(splits[2], (TAPS, C, C), (TAPS * C) ** -0.5, 0.109375)
    conv_two = centred(splits[3], (TAPS, C, C), (TAPS * C) ** -0.5, 0.109375)
    gain_one = jnp.clip(1.0 + 0.15 * jax.random.normal(splits[4], (C,), jnp.float32), 0.25, 1.75)
    shift_one = jnp.clip(jax.random.uniform(splits[5], (C,), jnp.float32, -0.6, 0.6), -0.6, 0.6)
    gain_two = jnp.clip(1.0 + 0.15 * jax.random.normal(splits[6], (C,), jnp.float32), 0.25, 1.75)
    shift_two = jnp.clip(jax.random.uniform(splits[7], (C,), jnp.float32, -0.6, 0.6), -0.6, 0.6)
    return dict(features=features, cotangent=cotangent, conv_one=conv_one, conv_two=conv_two, gain_one=gain_one, shift_one=shift_one, gain_two=gain_two, shift_two=shift_two)


epsilon = 1e-05

def unfold_taps(padded, frames, height, width):
    pieces = []
    for frame_off in range(3):
        for row_off in range(3):
            for col_off in range(3):
                pieces.append(padded[frame_off:frame_off + frames, row_off:row_off + height, col_off:col_off + width])
    stacked = jnp.concatenate(pieces, axis=3)
    return stacked.reshape(frames * height * width, stacked.shape[3])

def statistics(values):
    per_group = C // GROUPS
    members = FRAMES * HEIGHT * WIDTH * per_group
    grouped = values.reshape(-1, GROUPS, per_group)
    average = lax.optimization_barrier(jnp.sum(grouped, axis=(0, 2))) / members
    centered = grouped - average[None, :, None]
    variance = lax.optimization_barrier(jnp.sum(centered * centered, axis=(0, 2))) / members
    return (jnp.repeat(average, per_group), jnp.repeat(lax.rsqrt(variance + epsilon), per_group))

def group_means(first, second):
    per_group = C // GROUPS
    members = FRAMES * HEIGHT * WIDTH * per_group
    mean_first = lax.optimization_barrier(jnp.sum(first.reshape(-1, GROUPS, per_group), axis=(0, 2))) / members
    mean_second = lax.optimization_barrier(jnp.sum(second.reshape(-1, GROUPS, per_group), axis=(0, 2))) / members
    return (jnp.repeat(mean_first, per_group), jnp.repeat(mean_second, per_group))

def silu_slope(normed):
    sigm = jax.nn.sigmoid(normed)
    return sigm * (1.0 + normed * (1.0 - sigm))

def conv_frames(padded, kernel_flat):
    kernel_wide = kernel_flat.astype(jnp.float32)

    def one_frame(start):
        window = lax.dynamic_slice_in_dim(padded, start, 3, 0)
        columns = unfold_taps(window, 1, HEIGHT, WIDTH).astype(jnp.float32)
        return jnp.dot(columns, kernel_wide, precision=lax.Precision.HIGHEST)
    rows_out = lax.map(one_frame, jnp.arange(FRAMES, dtype=jnp.int32))
    return rows_out.reshape(FRAMES, HEIGHT, WIDTH, C)

def kernel_grad(padded, grad):

    def one_frame(carry, start):
        window = lax.dynamic_slice_in_dim(padded, start, 3, 0)
        columns = unfold_taps(window, 1, HEIGHT, WIDTH).astype(jnp.float32)
        frame_grad = lax.dynamic_index_in_dim(grad, start, 0, keepdims=False).reshape(HEIGHT * WIDTH, C).astype(jnp.float32)
        term = lax.dot_general(columns, frame_grad, (((0,), (0,)), ((), ())), precision=lax.Precision.HIGHEST)
        return (carry + term, None)
    summed, unused = lax.scan(one_frame, jnp.zeros((TAPS * C, C), jnp.float32), jnp.arange(FRAMES, dtype=jnp.int32))
    return summed.reshape(TAPS, C, C)

def pad_past(values):
    return jnp.pad(values, ((2, 0), (1, 1), (1, 1), (0, 0)))

def pad_future(values):
    return jnp.pad(values, ((0, 2), (1, 1), (1, 1), (0, 0)))

def flipped(kernel):
    return jnp.flip(kernel, 0).transpose(0, 2, 1).reshape(TAPS * C, C)

def reference(features, cotangent, conv_one, conv_two, gain_one, shift_one, gain_two, shift_two):
    inputs_wide = features.astype(jnp.float32)
    average_one, scale_one = statistics(inputs_wide)
    unit_one = (inputs_wide - average_one) * scale_one
    normed_one = unit_one * gain_one + shift_one
    acted_one = jax.nn.silu(normed_one).astype(jnp.bfloat16)
    padded_one = pad_past(acted_one)
    hidden = conv_frames(padded_one, conv_one.reshape(TAPS * C, C))
    average_two, scale_two = statistics(hidden)
    unit_two = (hidden - average_two) * scale_two
    normed_two = unit_two * gain_two + shift_two
    acted_two = jax.nn.silu(normed_two).astype(jnp.bfloat16)
    padded_two = pad_past(acted_two)
    block_out = (inputs_wide + conv_frames(padded_two, conv_two.reshape(TAPS * C, C))).astype(jnp.bfloat16)
    grad_conv_two = kernel_grad(padded_two, cotangent)
    back_two = conv_frames(pad_future(cotangent), flipped(conv_two))
    lifted_two = back_two * silu_slope(normed_two) * gain_two
    mean_first, mean_second = group_means(lifted_two, lifted_two * unit_two)
    grad_hidden = (scale_two * (lifted_two - mean_first - unit_two * mean_second)).astype(jnp.bfloat16)
    grad_conv_one = kernel_grad(padded_one, grad_hidden)
    back_one = conv_frames(pad_future(grad_hidden), flipped(conv_one))
    lifted_one = back_one * silu_slope(normed_one) * gain_one
    mean_first, mean_second = group_means(lifted_one, lifted_one * unit_one)
    grad_input = (cotangent.astype(jnp.float32) + scale_one * (lifted_one - mean_first - unit_one * mean_second)).astype(jnp.bfloat16)
    return (block_out, grad_input, grad_conv_one, grad_conv_two)
```

```python
import functools

import jax
import jax.numpy as jnp
from jax import lax
from jax.experimental import pallas as pl
from jax.experimental.pallas import tpu as pltpu
from jax.sharding import PartitionSpec as P

GROUPS = 32
EPSILON = 1e-05
MESH = pl.DeviceIdType.MESH
F32 = jnp.float32
BF16 = jnp.bfloat16
AXES = ("tm", "row", "col")


class Plan:
    def __init__(self, f, h, w, c, sizes):
        self.f, self.h, self.w, self.c = f, h, w, c
        self.wp = 16
        while self.wp < w + 2:
            self.wp *= 2
        self.n = f * h * self.wp
        self.hp = h + 2
        self.np = (f + 2) * self.hp * self.wp
        self.cb = -(-(f * h) // 16) * 16
        self.rb = 2 * self.wp
        self.ntm, self.nrow, self.ncol = sizes
        self.na = self.nrow
        self.nb = self.ntm * self.ncol


class Link:
    def __init__(self, src, dst, sems, index, device, sends, receives):
        self.make = lambda: pltpu.make_async_remote_copy(
            src_ref=src,
            dst_ref=dst,
            send_sem=sems[0].at[index],
            recv_sem=sems[1].at[index],
            device_id=device,
            device_id_type=MESH,
        )
        self.sends, self.receives = sends, receives

    def start(self):
        if self.sends is None:
            self.make().start()
            return

        @pl.when(self.sends)
        def _():
            self.make().start()

    def wait_send(self):
        if self.sends is None:
            self.make().wait_send()
            return

        @pl.when(self.sends)
        def _():
            self.make().wait_send()

    def wait_recv(self):
        if self.receives is None:
            self.make().wait_recv()
            return

        @pl.when(self.receives)
        def _():
            self.make().wait_recv()


class Place:
    def __init__(self, plan):
        self.t, self.r, self.c = (lax.axis_index(a) for a in AXES)
        self.has = dict(
            left=self.c > 0,
            right=self.c < plan.ncol - 1,
            up=self.r > 0,
            down=self.r < plan.nrow - 1,
            past=self.t > 0,
            future=self.t < plan.ntm - 1,
        )
        self.dev = dict(
            left={"col": self.c - 1},
            right={"col": self.c + 1},
            up={"row": self.r - 1},
            down={"row": self.r + 1},
            past={"tm": self.t - 1},
            future={"tm": self.t + 1},
        )

    def partners(self, plan):
        rows = [{"row": lax.rem(self.r + d, plan.na)} for d in range(1, plan.na)]
        index = self.t * plan.ncol + self.c
        others = []
        for d in range(1, plan.nb):
            to = lax.rem(index + d, plan.nb)
            others.append({"tm": lax.div(to, plan.ncol), "col": lax.rem(to, plan.ncol)})
        return rows, others


class Reduce:
    def __init__(self, plan, place, refs, sems, base):
        self.own, self.slots_a, self.mid, self.slots_b = refs
        rows, others = place.partners(plan)
        self.a = [
            Link(self.own, self.slots_a.at[d], sems, base + d, dev, None, None)
            for d, dev in enumerate(rows)
        ]
        self.b = [
            Link(self.mid, self.slots_b.at[d], sems, base + len(rows) + d, dev, None, None)
            for d, dev in enumerate(others)
        ]

    def start(self, first, second):
        self.own[...] = jnp.zeros_like(self.own)
        self.own[0:1] = first
        self.own[1:2] = second
        for link in self.a:
            link.start()

    def middle(self):
        for link in self.a:
            link.wait_recv()
        total = self.own[...]
        for d in range(len(self.a)):
            total = total + self.slots_a[d]
        self.mid[...] = total
        for link in self.b:
            link.start()

    def finish(self):
        for link in self.b:
            link.wait_recv()
        total = self.mid[...]
        for d in range(len(self.b)):
            total = total + self.slots_b[d]
        return total

    def drain(self):
        for link in self.a + self.b:
            link.wait_send()


EX_SEMS = 10


class Exchange:
    def __init__(self, plan, place, refs, sems, base, directions):
        self.plan, self.place, self.directions = plan, place, directions
        self.own, self.cols_out, self.cols_in, self.rows_out, self.rows_in = refs[:5]
        has, dev = place.has, place.dev
        cb, half = plan.cb, plan.f * plan.wp
        self.cols = [
            Link(self.cols_out.at[pl.ds(0, cb)], self.cols_in.at[pl.ds(0, cb)], sems, base,
                 dev["left"], has["left"], has["right"]),
            Link(self.cols_out.at[pl.ds(cb, cb)], self.cols_in.at[pl.ds(cb, cb)], sems, base + 1,
                 dev["right"], has["right"], has["left"]),
        ]
        self.rows = [
            Link(self.rows_out.at[pl.ds(0, half)], self.rows_in.at[pl.ds(half, half)], sems,
                 base + 2, dev["up"], has["up"], has["down"]),
            Link(self.rows_out.at[pl.ds(half, half)], self.rows_in.at[pl.ds(0, half)], sems,
                 base + 3, dev["down"], has["down"], has["up"]),
        ]
        self.tm = {}
        for k, source in enumerate(directions):
            block, cols, rows = refs[5 + 3 * k : 8 + 3 * k]
            target = "future" if source == "past" else "past"
            links = [
                Link(src, dst, sems, base + 4 + 3 * k + j, dev[target], has[target], has[source])
                for j, (src, dst) in enumerate(
                    [(self.own, block), (self.cols_in, cols), (self.rows_in, rows)]
                )
            ]
            self.tm[source] = ((block, cols, rows), links)

    def clear(self):
        cb, half = self.plan.cb, self.plan.f * self.plan.wp
        has = self.place.has

        def zero(ref, part, cond):
            @pl.when(jnp.logical_not(cond))
            def _():
                ref[part] = jnp.zeros(ref.at[part].shape, ref.dtype)

        zero(self.cols_in, pl.ds(0, cb), has["right"])
        zero(self.cols_in, pl.ds(cb, cb), has["left"])
        zero(self.rows_in, pl.ds(0, half), has["up"])
        zero(self.rows_in, pl.ds(half, half), has["down"])
        for source, (refs, _) in self.tm.items():
            for ref in refs:
                zero(ref, pl.ds(0, ref.shape[0]), has[source])

    def start(self, wide, pick):
        self.own[...] = wide[...].astype(BF16)
        for source in self.directions:
            self.tm[source][1][0].start()
        self.cols_out[...] = jnp.dot(pick[...], self.own[...], preferred_element_type=F32).astype(BF16)
        for link in self.cols:
            link.start()

    def middle(self, wide, spread):
        plan = self.plan
        for link in self.cols:
            link.wait_recv()
        for source in self.directions:
            self.tm[source][1][1].start()
        self.wide_ext = wide
        ends = spread_cols(self.cols_in, spread)
        size = plan.h * plan.wp
        for f in range(plan.f):
            for k, at in enumerate((f * size, (f + 1) * size - plan.wp)):
                self.rows_out[pl.ds((k * plan.f + f) * plan.wp, plan.wp)] = (
                    wide[pl.ds(at, plan.wp)] + ends[at : at + plan.wp]
                ).astype(BF16)
        for link in self.rows:
            link.start()

    def later(self):
        for link in self.rows:
            link.wait_recv()
        for source in self.directions:
            self.tm[source][1][2].start()

    def finish(self):
        for source in self.directions:
            for link in self.tm[source][1]:
                link.wait_recv()

    def drain(self):
        for link in self.cols + self.rows:
            link.wait_send()
        for source in self.directions:
            for link in self.tm[source][1]:
                link.wait_send()

    def pieces(self, wide, spread, source):
        plan = self.plan
        size = plan.h * plan.wp
        (block, cols, rows), _ = self.tm[source]

        def of(value, border, side):
            out = []
            for f in range(plan.f):
                top = border[pl.ds(f * plan.wp, plan.wp)].astype(F32)
                low = border[pl.ds((plan.f + f) * plan.wp, plan.wp)].astype(F32)
                out.append((side, top, value[f * size : (f + 1) * size], low))
            return out

        inner = of(wide[...] + spread_cols(self.cols_in, spread), self.rows_in, None)
        outer = of(block[...].astype(F32) + spread_cols(cols, spread), rows, source)
        if source == "past":
            return outer[plan.f - 2 :] + inner
        return inner + outer[:2]


def spread_cols(cols, spread):
    return jnp.dot(spread[...], cols[...], preferred_element_type=F32)


def silu(v):
    return v / (1.0 + jnp.exp(-v))


def slope(v):
    sigm = 1.0 / (1.0 + jnp.exp(-v))
    return sigm * (1.0 + v * (1.0 - sigm))


def valid(plan, place, count, side, border):
    has = place.has
    w = lax.broadcasted_iota(jnp.int32, (count, plan.c), 0) & (plan.wp - 1)
    one = lambda cond: cond.astype(jnp.int32)
    mask = jnp.where(
        w < plan.w,
        1,
        jnp.where(
            w == plan.w,
            one(has["right"]),
            jnp.where(w == plan.wp - 1, one(has["left"]), 0),
        ),
    )
    for name in (side, border):
        if name is not None:
            mask = mask * one(has[name])
    return mask > 0


def store_shifted(plan, ref, at, value):
    count = value.shape[0]
    rows = value.reshape(count // plan.wp, plan.wp, plan.c)
    before = pltpu.roll(rows, 1, axis=1).reshape(value.shape)
    after = pltpu.roll(rows, plan.wp - 1, axis=1).reshape(value.shape)
    c = plan.c
    ref[pl.ds(at, count), 0:c] = before.astype(BF16)
    ref[pl.ds(at, count), c : 2 * c] = value.astype(BF16)
    ref[pl.ds(at, count), 2 * c : 3 * c] = after.astype(BF16)


def build(plan, ref, frames):
    for k, (top, rows, low) in enumerate(frames):
        at = k * plan.hp * plan.wp
        store_shifted(plan, ref, at, top)
        store_shifted(plan, ref, at + plan.wp, rows)
        store_shifted(plan, ref, at + (plan.h + 1) * plan.wp, low)


def convolve(plan, ref, kernel, out):
    size = plan.h * plan.wp

    def frame(f, carry):
        pieces = []
        for p in range(3):
            for q in range(3):
                at = pl.multiple_of(((f + p) * plan.hp + q) * plan.wp, plan.wp)
                pieces.append(ref[pl.ds(at, size), :])
        wide = jnp.dot(jnp.concatenate(pieces, axis=1), kernel[...], preferred_element_type=F32)
        w = lax.broadcasted_iota(jnp.int32, wide.shape, 0) & (plan.wp - 1)
        out[pl.ds(pl.multiple_of(f * size, size), size), :] = jnp.where(w < plan.w, wide, 0.0)
        return carry

    lax.fori_loop(0, plan.f, frame, 0)


def kernel_term(plan, ref, grad, part):
    size = plan.h * plan.wp
    turned = grad.T.astype(BF16)

    def tap(pq, carry):
        p, q = lax.div(pq, 3), lax.rem(pq, 3)
        pieces = []
        for f in range(plan.f):
            at = pl.multiple_of(((f + p) * plan.hp + q) * plan.wp, plan.wp)
            pieces.append(ref[pl.ds(at, size), :])
        term = jnp.dot(turned, jnp.concatenate(pieces, axis=0), preferred_element_type=F32)
        part[pl.ds(pl.multiple_of(pq * 3 * plan.c, 3 * plan.c), 3 * plan.c), :] = term.T
        return carry

    lax.fori_loop(0, 9, tap, 0)


def turn_kernel(plan, kernel, out):
    taps, c = 27, plan.c

    def tap(k, carry):
        source = kernel[pl.ds(pl.multiple_of((taps - 1 - k) * c, c), c), :]
        out[pl.ds(pl.multiple_of(k * c, c), c), :] = source.astype(F32).T.astype(BF16)
        return carry

    lax.fori_loop(0, taps, tap, 0)


def spaced(plan, ref, wide):
    wide[...] = jnp.zeros_like(wide)
    for f in range(plan.f):
        for y in range(plan.h):
            wide[pl.ds((f * plan.h + y) * plan.wp, plan.w)] = ref[f, y].astype(F32)


def unspaced(plan, value, ref):
    for f in range(plan.f):
        for y in range(plan.h):
            at = (f * plan.h + y) * plan.wp
            ref[f, y] = value[at : at + plan.w].astype(BF16)


def column_sum(value):
    return jnp.sum(value, axis=0, keepdims=True)


def body(plan, n_ex, *refs):
    refs = list(refs)
    take = lambda k: [refs.pop(0) for _ in range(k)]
    features, cotangent, kernel_one, kernel_two, norms = take(5)
    block_out, grad_input, part_one, part_two = take(4)
    wide_x, wide_g, wide_h, wide_l, wide_b = take(5)
    pick, spread, turned_one, turned_two = take(4)
    x3_one, x3_two, x3_g, x3_h = take(4)
    exchange_refs = [take(k) for k in n_ex]
    reduce_refs = [take(4) for _ in range(4)]
    sems = take(2)

    place = Place(plan)
    rows, others = place.partners(plan)
    per_reduce = len(rows) + len(others)
    exchanges = [
        Exchange(plan, place, r, sems, EX_SEMS * k, d)
        for k, (r, d) in enumerate(
            zip(exchange_refs, (("past",), ("future",), ("past", "future"), ("future",)))
        )
    ]
    ex_x, ex_g, ex_h, ex_l = exchanges
    reduces = [
        Reduce(plan, place, r, sems, EX_SEMS * 4 + per_reduce * k)
        for k, r in enumerate(reduce_refs)
    ]
    for ex in exchanges:
        ex.clear()

    barrier = pltpu.get_barrier_semaphore()
    for dev in rows + others:
        pl.semaphore_signal(barrier, inc=1, device_id=dev, device_id_type=MESH)

    c = plan.c
    per_group = c // GROUPS
    members = float(plan.f * plan.h * plan.w * plan.ntm * plan.nrow * plan.ncol * per_group)
    lane_i = lax.broadcasted_iota(jnp.int32, (c, c), 0)
    lane_j = lax.broadcasted_iota(jnp.int32, (c, c), 1)
    same = (lax.div(lane_i, per_group) == lax.div(lane_j, per_group)).astype(F32)

    def group_means(total):
        sums = jnp.dot(
            total, same, preferred_element_type=F32, precision=lax.Precision.HIGHEST
        )
        return sums[0:1] / members, sums[1:2] / members

    def moments(total):
        average, square = group_means(total)
        return average, lax.rsqrt(square - average * average + EPSILON)

    spaced(plan, features, wide_x)
    j = lax.broadcasted_iota(jnp.int32, (2 * plan.cb, plan.n), 0)
    at = lax.broadcasted_iota(jnp.int32, (2 * plan.cb, plan.n), 1)
    first = j < plan.cb
    pick[...] = (
        at == jnp.where(first, j * plan.wp, (j - plan.cb) * plan.wp + plan.w - 1)
    ).astype(F32).astype(BF16)
    at = lax.broadcasted_iota(jnp.int32, (plan.n, 2 * plan.cb), 0)
    j = lax.broadcasted_iota(jnp.int32, (plan.n, 2 * plan.cb), 1)
    first = j < plan.cb
    spread[...] = (
        at == jnp.where(first, j * plan.wp + plan.w, (j - plan.cb) * plan.wp + plan.wp - 1)
    ).astype(F32).astype(BF16)

    pl.semaphore_wait(barrier, per_reduce)
    gain_one, shift_one = norms[0:1], norms[1:2]
    gain_two, shift_two = norms[2:3], norms[3:4]

    x = wide_x[...]
    reduces[0].start(column_sum(x), column_sum(x * x))
    ex_x.start(wide_x, pick)
    spaced(plan, cotangent, wide_g)
    ex_g.start(wide_g, pick)
    reduces[0].middle()
    ex_x.middle(wide_x, spread)
    ex_g.middle(wide_g, spread)
    turn_kernel(plan, kernel_two, turned_two)
    ex_x.later()
    ex_g.later()
    turn_kernel(plan, kernel_one, turned_one)
    mean_one, scale_one = moments(reduces[0].finish())
    ex_x.finish()

    def unit_one(v):
        return (v - mean_one) * scale_one

    def frames_of(pieces, fn):
        out = []
        for side, top, rows_, low in pieces:
            keep = lambda v, border: jnp.where(
                valid(plan, place, v.shape[0], side, border), fn(v), 0.0
            )
            out.append((keep(top, "up"), keep(rows_, None), keep(low, "down")))
        return out

    build(
        plan,
        x3_one,
        frames_of(
            ex_x.pieces(wide_x, spread, "past"),
            lambda v: silu(unit_one(v) * gain_one + shift_one),
        ),
    )
    convolve(plan, x3_one, kernel_one, wide_h)
    hidden = wide_h[...]
    reduces[1].start(column_sum(hidden), column_sum(hidden * hidden))
    ex_h.start(wide_h, pick)
    reduces[1].middle()
    ex_h.middle(wide_h, spread)
    ex_g.finish()
    build(plan, x3_g, [p[1:] for p in ex_g.pieces(wide_g, spread, "future")])
    ex_h.later()
    convolve(plan, x3_g, turned_two, wide_b)
    mean_two, scale_two = moments(reduces[1].finish())

    def unit_two(v):
        return (v - mean_two) * scale_two

    unit = unit_two(wide_h[...])
    lifted = wide_b[...] * slope(unit * gain_two + shift_two) * gain_two
    wide_l[...] = lifted
    reduces[2].start(column_sum(lifted), column_sum(lifted * unit))
    ex_l.start(wide_l, pick)
    reduces[2].middle()
    ex_l.middle(wide_l, spread)
    ex_h.finish()
    build(
        plan,
        x3_two,
        frames_of(
            ex_h.pieces(wide_h, spread, "past"),
            lambda v: silu(unit_two(v) * gain_two + shift_two),
        ),
    )
    ex_l.later()
    kernel_term(plan, x3_two, wide_g[...], part_two)
    convolve(plan, x3_two, kernel_two, wide_b)
    unspaced(plan, wide_x[...] + wide_b[...], block_out)

    a_two, b_two = group_means(reduces[2].finish())
    ex_l.finish()
    frames = []
    for (side, *lifts), (_, *hids) in zip(
        ex_l.pieces(wide_l, spread, "future"), ex_h.pieces(wide_h, spread, "future")
    ):
        out = []
        for border, lift, hid in zip(("up", None, "down"), lifts, hids):
            value = scale_two * (lift - a_two - unit_two(hid) * b_two)
            out.append(jnp.where(valid(plan, place, lift.shape[0], side, border), value, 0.0))
        frames.append(tuple(out))
    build(plan, x3_h, frames)
    convolve(plan, x3_h, turned_one, wide_b)
    unit = unit_one(wide_x[...])
    lifted = wide_b[...] * slope(unit * gain_one + shift_one) * gain_one
    reduces[3].start(column_sum(lifted), column_sum(lifted * unit))
    wide_l[...] = lifted
    reduces[3].middle()
    w = lax.broadcasted_iota(jnp.int32, (plan.h * plan.wp, c), 0) & (plan.wp - 1)
    own = jnp.concatenate(
        [jnp.where(w < plan.w, frames[f][1], 0.0) for f in range(plan.f)], axis=0
    )
    kernel_term(plan, x3_one, own, part_one)
    a_one, b_one = group_means(reduces[3].finish())
    unit = unit_one(wide_x[...])
    unspaced(
        plan,
        wide_g[...] + scale_one * (wide_l[...] - a_one - unit * b_one),
        grad_input,
    )
    for item in exchanges + reduces:
        item.drain()


def block_kernel(plan, features, cotangent, kernel_one, kernel_two, norms):
    c, n = plan.c, plan.n
    half = plan.f * plan.wp
    exchange = []
    n_ex = []
    for count in (1, 1, 2, 1):
        shapes = [(n, c), (2 * plan.cb, c), (2 * plan.cb, c), (2 * half, c), (2 * half, c)]
        shapes += [(n, c), (2 * plan.cb, c), (2 * half, c)] * count
        n_ex.append(len(shapes))
        exchange += [pltpu.VMEM(s, BF16) for s in shapes]
    reduce = [
        pltpu.VMEM((8, c), F32),
        pltpu.VMEM((max(1, plan.na - 1), 8, c), F32),
        pltpu.VMEM((8, c), F32),
        pltpu.VMEM((max(1, plan.nb - 1), 8, c), F32),
    ] * 4
    sems = 4 * EX_SEMS + 4 * (plan.na + plan.nb - 2)
    vmem = pl.BlockSpec(memory_space=pltpu.VMEM)
    taps = kernel_one.shape[0]
    return pl.pallas_call(
        functools.partial(body, plan, n_ex),
        out_shape=(
            jax.ShapeDtypeStruct(features.shape, BF16),
            jax.ShapeDtypeStruct(features.shape, BF16),
            jax.ShapeDtypeStruct((taps, c), F32),
            jax.ShapeDtypeStruct((taps, c), F32),
        ),
        in_specs=[vmem] * 5,
        out_specs=(vmem,) * 4,
        scratch_shapes=[pltpu.VMEM((n, c), F32)] * 5
        + [pltpu.VMEM((2 * plan.cb, n), BF16), pltpu.VMEM((n, 2 * plan.cb), BF16)]
        + [pltpu.VMEM((taps, c), BF16)] * 2
        + [pltpu.VMEM((plan.np, 3 * c), BF16)] * 4
        + exchange
        + reduce
        + [pltpu.SemaphoreType.DMA((sems,))] * 2,
        compiler_params=pltpu.CompilerParams(
            collective_id=0, has_side_effects=True, vmem_limit_bytes=52 * 2**20
        ),
    )(features, cotangent, kernel_one, kernel_two, norms)


def local(features, cotangent, conv_one, conv_two, gain_one, shift_one, gain_two, shift_two):
    f, h, w, c = features.shape
    plan = Plan(f, h, w, c, tuple(lax.axis_size(a) for a in AXES))
    norms = jnp.stack([gain_one, shift_one, gain_two, shift_two])
    block_out, grad_input, part_one, part_two = block_kernel(
        plan, features, cotangent, conv_one.reshape(-1, c), conv_two.reshape(-1, c), norms
    )
    sum_one, sum_two = lax.psum((part_one, part_two), AXES)
    return block_out, grad_input, sum_one.reshape(conv_one.shape), sum_two.reshape(conv_two.shape)


def solution(mesh):
    block = P("tm", "row", "col", None)
    return jax.shard_map(
        local,
        mesh=mesh,
        in_specs=(block, block) + (P(),) * 6,
        out_specs=(block, block, P(), P()),
        check_vma=False,
    )
```

```python
import functools

import jax
import jax.numpy as jnp
from jax import lax
from jax.experimental import pallas as pl
from jax.experimental.pallas import tpu as pltpu
from jax.sharding import PartitionSpec as P

GROUPS = 32
EPSILON = 1e-05
MESH = pl.DeviceIdType.MESH
F32 = jnp.float32
BF16 = jnp.bfloat16
AXES = ("tm", "row", "col")


class Plan:
    def __init__(self, f, h, w, c, sizes):
        self.f, self.h, self.w, self.c = f, h, w, c
        self.wp = 16
        while self.wp < w + 2:
            self.wp *= 2
        self.n = f * h * self.wp
        self.hp = h + 2
        self.np = (f + 2) * self.hp * self.wp
        self.cb = -(-(f * h) // 16) * 16
        self.rb = 2 * self.wp
        self.ntm, self.nrow, self.ncol = sizes
        self.na = self.nrow
        self.nb = self.ntm * self.ncol
        self.taps_rows = 27 * c
        unit = 16 * self.ntm * self.nrow * self.ncol
        units = -(-self.taps_rows // unit)
        first = -(-units // 2)
        self.sum_rows = units * unit
        self.parts = [(0, first * unit)]
        if units > first:
            self.parts.append((first * unit, (units - first) * unit))

    def stages(self, order):
        near = 2 if self.ncol % 2 == 0 else 1
        known = dict(
            near=("col", 1, near, True),
            col=("col", near, self.ncol // near, False),
            tm=("tm", 1, self.ntm, False),
            row=("row", 1, self.nrow, True),
        )
        return [known[name] for name in order if known[name][2] > 1]


class Link:
    def __init__(self, src, dst, sems, index, device, sends, receives):
        self.make = lambda: pltpu.make_async_remote_copy(
            src_ref=src,
            dst_ref=dst,
            send_sem=sems[0].at[index],
            recv_sem=sems[1].at[index],
            device_id=device,
            device_id_type=MESH,
        )
        self.sends, self.receives = sends, receives

    def start(self):
        if self.sends is None:
            self.make().start()
            return

        @pl.when(self.sends)
        def _():
            self.make().start()

    def wait_send(self):
        if self.sends is None:
            self.make().wait_send()
            return

        @pl.when(self.sends)
        def _():
            self.make().wait_send()

    def wait_recv(self):
        if self.receives is None:
            self.make().wait_recv()
            return

        @pl.when(self.receives)
        def _():
            self.make().wait_recv()


class Place:
    def __init__(self, plan):
        self.t, self.r, self.c = (lax.axis_index(a) for a in AXES)
        self.has = dict(
            left=self.c > 0,
            right=self.c < plan.ncol - 1,
            up=self.r > 0,
            down=self.r < plan.nrow - 1,
            past=self.t > 0,
            future=self.t < plan.ntm - 1,
        )
        self.dev = dict(
            left={"col": self.c - 1},
            right={"col": self.c + 1},
            up={"row": self.r - 1},
            down={"row": self.r + 1},
            past={"tm": self.t - 1},
            future={"tm": self.t + 1},
        )

    def partners(self, plan):
        rows = [{"row": lax.rem(self.r + d, plan.na)} for d in range(1, plan.na)]
        index = self.t * plan.ncol + self.c
        others = []
        for d in range(1, plan.nb):
            to = lax.rem(index + d, plan.nb)
            others.append({"tm": lax.div(to, plan.ncol), "col": lax.rem(to, plan.ncol)})
        return rows, others


class Reduce:
    def __init__(self, plan, place, refs, sems, base):
        self.own, self.slots_a, self.mid, self.slots_b = refs
        rows, others = place.partners(plan)
        self.a = [
            Link(self.own, self.slots_a.at[d], sems, base + d, dev, None, None)
            for d, dev in enumerate(rows)
        ]
        self.b = [
            Link(self.mid, self.slots_b.at[d], sems, base + len(rows) + d, dev, None, None)
            for d, dev in enumerate(others)
        ]

    def start(self, first, second):
        self.own[...] = jnp.zeros_like(self.own)
        self.own[0:1] = first
        self.own[1:2] = second
        for link in self.a:
            link.start()

    def middle(self):
        for link in self.a:
            link.wait_recv()
        total = self.own[...]
        for d in range(len(self.a)):
            total = total + self.slots_a[d]
        self.mid[...] = total
        for link in self.b:
            link.start()

    def finish(self):
        for link in self.b:
            link.wait_recv()
        total = self.mid[...]
        for d in range(len(self.b)):
            total = total + self.slots_b[d]
        return total

    def drain(self):
        for link in self.a + self.b:
            link.wait_send()


class KernelSum:
    def __init__(self, plan, place, stages, span, acc, done, outs, ins, sems, base):
        self.acc, self.done, self.outs, self.ins = acc, done, outs, ins
        self.stages = stages
        at, count = span
        self.spans, self.reduce, self.gather = [], [], []
        for k, (axis, stride, ways, wide) in enumerate(stages):
            here = dict(tm=place.t, row=place.r, col=place.c)[axis]
            mine = lax.rem(lax.div(here, stride), ways)
            piece = count // ways
            aligned = lambda v: pl.multiple_of(v, 16)
            kept = aligned(at + mine * piece)
            links, sources = [], []
            for d in range(1, ways):
                other = lax.rem(mine + d, ways)
                dev = {axis: here + (other - mine) * stride}
                sent = aligned(at + other * piece)
                if wide:
                    src = acc.at[pl.ds(sent, piece)]
                else:
                    src = outs[k].at[d - 1]
                    sources.append((d - 1, sent))
                links.append((Link(src, ins[k].at[d - 1], sems, base, dev, None, None), dev))
                base += 1
            self.reduce.append([link for link, _ in links])
            gathers = []
            for _, dev in links:
                part = done.at[pl.ds(kept, piece)]
                gathers.append(Link(part, part, sems, base, dev, None, None))
                base += 1
            self.gather.append(gathers)
            self.spans.append((kept, piece, sources))
            at, count = kept, piece
        self.base = base

    def steps(self):
        out = []
        last = len(self.stages) - 1
        for k in range(len(self.stages)):
            out.append(functools.partial(self.reduce_step, k))
        for k in range(last, -1, -1):
            out.append(functools.partial(self.gather_step, k))
        out.append(self.last_step)
        return out

    def reduce_step(self, k):
        if k:
            self.settle(k - 1)
        kept, piece, sources = self.spans[k]
        for slot, sent in sources:
            self.outs[k][slot] = self.acc[pl.ds(sent, piece)].astype(BF16)
        for link in self.reduce[k]:
            link.start()

    def settle(self, k):
        kept, piece, _ = self.spans[k]
        for link in self.reduce[k]:
            link.wait_recv()
        total = self.acc[pl.ds(kept, piece)]
        for d in range(len(self.reduce[k])):
            total = total + self.ins[k][d].astype(F32)
        if k == len(self.stages) - 1:
            self.done[pl.ds(kept, piece)] = total.astype(BF16)
        else:
            self.acc[pl.ds(kept, piece)] = total

    def gather_step(self, k):
        if k == len(self.stages) - 1:
            self.settle(k)
        else:
            for link in self.gather[k + 1]:
                link.wait_recv()
        for link in self.gather[k]:
            link.start()

    def last_step(self):
        for link in self.gather[0]:
            link.wait_recv()

    def drain(self):
        for links in self.reduce + self.gather:
            for link in links:
                link.wait_send()


ORDERS = (("near", "col", "tm", "row"), ("near", "tm", "col", "row"))


def sum_scratch(plan):
    shapes, counts = [], []
    for order, (_, count) in zip(ORDERS, plan.parts):
        outs, ins = [], []
        for axis, stride, ways, wide in plan.stages(order):
            piece = count // ways
            shape = (ways - 1, piece, plan.c)
            outs.append(pltpu.VMEM((1, 16, plan.c) if wide else shape, BF16))
            ins.append(pltpu.VMEM(shape, F32 if wide else BF16))
            count = piece
        counts.append(len(outs))
        shapes += outs + ins
    return shapes, counts


def sum_sems(plan):
    return 2 * sum(
        stage[2] - 1 for order, _ in zip(ORDERS, plan.parts) for stage in plan.stages(order)
    )


EX_SEMS = 10


class Exchange:
    def __init__(self, plan, place, refs, sems, base, directions):
        self.plan, self.place, self.directions = plan, place, directions
        self.own, self.cols_out, self.cols_in, self.rows_out, self.rows_in = refs[:5]
        has, dev = place.has, place.dev
        cb, half = plan.cb, plan.f * plan.wp
        self.cols = [
            Link(self.cols_out.at[pl.ds(0, cb)], self.cols_in.at[pl.ds(0, cb)], sems, base,
                 dev["left"], has["left"], has["right"]),
            Link(self.cols_out.at[pl.ds(cb, cb)], self.cols_in.at[pl.ds(cb, cb)], sems, base + 1,
                 dev["right"], has["right"], has["left"]),
        ]
        self.rows = [
            Link(self.rows_out.at[pl.ds(0, half)], self.rows_in.at[pl.ds(half, half)], sems,
                 base + 2, dev["up"], has["up"], has["down"]),
            Link(self.rows_out.at[pl.ds(half, half)], self.rows_in.at[pl.ds(0, half)], sems,
                 base + 3, dev["down"], has["down"], has["up"]),
        ]
        self.tm = {}
        for k, source in enumerate(directions):
            block, cols, rows = refs[5 + 3 * k : 8 + 3 * k]
            target = "future" if source == "past" else "past"
            links = [
                Link(src, dst, sems, base + 4 + 3 * k + j, dev[target], has[target], has[source])
                for j, (src, dst) in enumerate(
                    [(self.own, block), (self.cols_in, cols), (self.rows_in, rows)]
                )
            ]
            self.tm[source] = ((block, cols, rows), links)

    def clear(self):
        cb, half = self.plan.cb, self.plan.f * self.plan.wp
        has = self.place.has

        def zero(ref, part, cond):
            @pl.when(jnp.logical_not(cond))
            def _():
                ref[part] = jnp.zeros(ref.at[part].shape, ref.dtype)

        zero(self.cols_in, pl.ds(0, cb), has["right"])
        zero(self.cols_in, pl.ds(cb, cb), has["left"])
        zero(self.rows_in, pl.ds(0, half), has["up"])
        zero(self.rows_in, pl.ds(half, half), has["down"])
        for source, (refs, _) in self.tm.items():
            for ref in refs:
                zero(ref, pl.ds(0, ref.shape[0]), has[source])

    def start(self, wide, pick):
        self.own[...] = wide[...].astype(BF16)
        for source in self.directions:
            self.tm[source][1][0].start()
        self.cols_out[...] = jnp.dot(pick[...], self.own[...], preferred_element_type=F32).astype(BF16)
        for link in self.cols:
            link.start()

    def middle(self, wide, spread):
        plan = self.plan
        for link in self.cols:
            link.wait_recv()
        for source in self.directions:
            self.tm[source][1][1].start()
        ends = spread_cols(self.cols_in, spread)
        size = plan.h * plan.wp
        for f in range(plan.f):
            for k, at in enumerate((f * size, (f + 1) * size - plan.wp)):
                self.rows_out[pl.ds((k * plan.f + f) * plan.wp, plan.wp)] = (
                    wide[pl.ds(at, plan.wp)] + ends[at : at + plan.wp]
                ).astype(BF16)
        for link in self.rows:
            link.start()

    def later(self):
        for link in self.rows:
            link.wait_recv()
        for source in self.directions:
            self.tm[source][1][2].start()

    def finish(self):
        for source in self.directions:
            for link in self.tm[source][1]:
                link.wait_recv()

    def drain(self):
        for link in self.cols + self.rows:
            link.wait_send()
        for source in self.directions:
            for link in self.tm[source][1]:
                link.wait_send()

    def pieces(self, wide, spread, source):
        plan = self.plan
        size = plan.h * plan.wp
        (block, cols, rows), _ = self.tm[source]

        def of(value, border, side):
            out = []
            for f in range(plan.f):
                top = border[pl.ds(f * plan.wp, plan.wp)].astype(F32)
                low = border[pl.ds((plan.f + f) * plan.wp, plan.wp)].astype(F32)
                out.append((side, top, value[f * size : (f + 1) * size], low))
            return out

        inner = of(wide[...] + spread_cols(self.cols_in, spread), self.rows_in, None)
        outer = of(block[...].astype(F32) + spread_cols(cols, spread), rows, source)
        if source == "past":
            return outer[plan.f - 2 :] + inner
        return inner + outer[:2]


def spread_cols(cols, spread):
    return jnp.dot(spread[...], cols[...], preferred_element_type=F32)


def silu(v):
    return v / (1.0 + jnp.exp(-v))


def slope(v):
    sigm = 1.0 / (1.0 + jnp.exp(-v))
    return sigm * (1.0 + v * (1.0 - sigm))


def valid(plan, place, count, side, border):
    has = place.has
    w = lax.broadcasted_iota(jnp.int32, (count, plan.c), 0) & (plan.wp - 1)
    one = lambda cond: cond.astype(jnp.int32)
    mask = jnp.where(
        w < plan.w,
        1,
        jnp.where(
            w == plan.w,
            one(has["right"]),
            jnp.where(w == plan.wp - 1, one(has["left"]), 0),
        ),
    )
    for name in (side, border):
        if name is not None:
            mask = mask * one(has[name])
    return mask > 0


def store_shifted(plan, ref, at, value):
    count = value.shape[0]
    rows = value.reshape(count // plan.wp, plan.wp, plan.c)
    before = pltpu.roll(rows, 1, axis=1).reshape(value.shape)
    after = pltpu.roll(rows, plan.wp - 1, axis=1).reshape(value.shape)
    c = plan.c
    ref[pl.ds(at, count), 0:c] = before.astype(BF16)
    ref[pl.ds(at, count), c : 2 * c] = value.astype(BF16)
    ref[pl.ds(at, count), 2 * c : 3 * c] = after.astype(BF16)


def build(plan, ref, frames):
    for k, (top, rows, low) in enumerate(frames):
        at = k * plan.hp * plan.wp
        store_shifted(plan, ref, at, top)
        store_shifted(plan, ref, at + plan.wp, rows)
        store_shifted(plan, ref, at + (plan.h + 1) * plan.wp, low)


def convolve(plan, ref, kernel, out):
    size = plan.h * plan.wp

    def frame(f, carry):
        pieces = []
        for p in range(3):
            for q in range(3):
                at = pl.multiple_of(((f + p) * plan.hp + q) * plan.wp, plan.wp)
                pieces.append(ref[pl.ds(at, size), :])
        wide = jnp.dot(jnp.concatenate(pieces, axis=1), kernel[...], preferred_element_type=F32)
        w = lax.broadcasted_iota(jnp.int32, wide.shape, 0) & (plan.wp - 1)
        out[pl.ds(pl.multiple_of(f * size, size), size), :] = jnp.where(w < plan.w, wide, 0.0)
        return carry

    lax.fori_loop(0, plan.f, frame, 0)


def kernel_term(plan, ref, turned, part, low, high):
    size = plan.h * plan.wp

    def tap(pq, carry):
        p, q = lax.div(pq, 3), lax.rem(pq, 3)
        pieces = []
        for f in range(plan.f):
            at = pl.multiple_of(((f + p) * plan.hp + q) * plan.wp, plan.wp)
            pieces.append(ref[pl.ds(at, size), :])
        term = jnp.dot(turned, jnp.concatenate(pieces, axis=0), preferred_element_type=F32)
        part[pl.ds(pl.multiple_of(pq * 3 * plan.c, 3 * plan.c), 3 * plan.c), :] = term.T
        return carry

    lax.fori_loop(low, high, tap, 0)


def turn_kernel(plan, kernel, out):
    taps, c = 27, plan.c

    def tap(k, carry):
        source = kernel[pl.ds(pl.multiple_of((taps - 1 - k) * c, c), c), :]
        out[pl.ds(pl.multiple_of(k * c, c), c), :] = source.astype(F32).T.astype(BF16)
        return carry

    lax.fori_loop(0, taps, tap, 0)


def spaced(plan, ref, wide):
    wide[...] = jnp.zeros_like(wide)
    for f in range(plan.f):
        for y in range(plan.h):
            wide[pl.ds((f * plan.h + y) * plan.wp, plan.w)] = ref[f, y].astype(F32)


def unspaced(plan, value, ref):
    for f in range(plan.f):
        for y in range(plan.h):
            at = (f * plan.h + y) * plan.wp
            ref[f, y] = value[at : at + plan.w].astype(BF16)


def column_sum(value):
    return jnp.sum(value, axis=0, keepdims=True)


def body(plan, n_ex, *refs):
    refs = list(refs)
    take = lambda k: [refs.pop(0) for _ in range(k)]
    features, cotangent, kernel_one, kernel_two, norms = take(5)
    block_out, grad_input, part_one, part_two = take(4)
    wide_x, wide_g, wide_h, wide_l, wide_b = take(5)
    pick, spread, turned_one, turned_two = take(4)
    x3_one, x3_two, x3_g, x3_h = take(4)
    exchange_refs = [take(k) for k in n_ex]
    reduce_refs = [take(4) for _ in range(4)]
    acc_one, acc_two, done_one, done_two = take(4)
    sum_refs = []
    for _ in range(2):
        for count in sum_scratch(plan)[1]:
            sum_refs.append((take(count), take(count)))
    sems = take(2)

    place = Place(plan)
    rows, others = place.partners(plan)
    per_reduce = len(rows) + len(others)
    exchanges = [
        Exchange(plan, place, r, sems, EX_SEMS * k, d)
        for k, (r, d) in enumerate(
            zip(exchange_refs, (("past",), ("future",), ("past", "future"), ("future",)))
        )
    ]
    ex_x, ex_g, ex_h, ex_l = exchanges
    reduces = [
        Reduce(plan, place, r, sems, EX_SEMS * 4 + per_reduce * k)
        for k, r in enumerate(reduce_refs)
    ]
    sums = []
    base = EX_SEMS * 4 + per_reduce * 4
    for acc, done in ((acc_two, done_two), (acc_one, done_one)):
        for order, span in zip(ORDERS, plan.parts):
            outs, ins = sum_refs[len(sums)]
            sums.append(
                KernelSum(plan, place, plan.stages(order), span, acc, done, outs, ins, sems, base)
            )
            base = sums[-1].base
        acc[pl.ds(plan.taps_rows, plan.sum_rows - plan.taps_rows)] = jnp.zeros(
            (plan.sum_rows - plan.taps_rows, plan.c), F32
        )
    sums_two, sums_one = sums[: len(plan.parts)], sums[len(plan.parts) :]
    steps_two = [list(group) for group in zip(*[item.steps() for item in sums_two])]

    def advance():
        if steps_two:
            for step in steps_two.pop(0):
                step()

    for ex in exchanges:
        ex.clear()

    barrier = pltpu.get_barrier_semaphore()
    for dev in rows + others:
        pl.semaphore_signal(barrier, inc=1, device_id=dev, device_id_type=MESH)

    c = plan.c
    per_group = c // GROUPS
    members = float(plan.f * plan.h * plan.w * plan.ntm * plan.nrow * plan.ncol * per_group)
    lane_i = lax.broadcasted_iota(jnp.int32, (c, c), 0)
    lane_j = lax.broadcasted_iota(jnp.int32, (c, c), 1)
    same = (lax.div(lane_i, per_group) == lax.div(lane_j, per_group)).astype(F32)

    def group_means(total):
        sums = jnp.dot(
            total, same, preferred_element_type=F32, precision=lax.Precision.HIGHEST
        )
        return sums[0:1] / members, sums[1:2] / members

    def moments(total):
        average, square = group_means(total)
        return average, lax.rsqrt(square - average * average + EPSILON)

    spaced(plan, features, wide_x)
    j = lax.broadcasted_iota(jnp.int32, (2 * plan.cb, plan.n), 0)
    at = lax.broadcasted_iota(jnp.int32, (2 * plan.cb, plan.n), 1)
    first = j < plan.cb
    pick[...] = (
        at == jnp.where(first, j * plan.wp, (j - plan.cb) * plan.wp + plan.w - 1)
    ).astype(F32).astype(BF16)
    at = lax.broadcasted_iota(jnp.int32, (plan.n, 2 * plan.cb), 0)
    j = lax.broadcasted_iota(jnp.int32, (plan.n, 2 * plan.cb), 1)
    first = j < plan.cb
    spread[...] = (
        at == jnp.where(first, j * plan.wp + plan.w, (j - plan.cb) * plan.wp + plan.wp - 1)
    ).astype(F32).astype(BF16)

    pl.semaphore_wait(barrier, per_reduce)
    gain_one, shift_one = norms[0:1], norms[1:2]
    gain_two, shift_two = norms[2:3], norms[3:4]

    x = wide_x[...]
    reduces[0].start(column_sum(x), column_sum(x * x))
    ex_x.start(wide_x, pick)
    spaced(plan, cotangent, wide_g)
    ex_g.start(wide_g, pick)
    reduces[0].middle()
    ex_x.middle(wide_x, spread)
    ex_g.middle(wide_g, spread)
    turn_kernel(plan, kernel_two, turned_two)
    ex_x.later()
    ex_g.later()
    turn_kernel(plan, kernel_one, turned_one)
    mean_one, scale_one = moments(reduces[0].finish())
    ex_x.finish()

    def unit_one(v):
        return (v - mean_one) * scale_one

    def frames_of(pieces, fn):
        out = []
        for side, top, rows_, low in pieces:
            keep = lambda v, border: jnp.where(
                valid(plan, place, v.shape[0], side, border), fn(v), 0.0
            )
            out.append((keep(top, "up"), keep(rows_, None), keep(low, "down")))
        return out

    build(
        plan,
        x3_one,
        frames_of(
            ex_x.pieces(wide_x, spread, "past"),
            lambda v: silu(unit_one(v) * gain_one + shift_one),
        ),
    )
    convolve(plan, x3_one, kernel_one, wide_h)
    hidden = wide_h[...]
    reduces[1].start(column_sum(hidden), column_sum(hidden * hidden))
    ex_h.start(wide_h, pick)
    reduces[1].middle()
    ex_h.middle(wide_h, spread)
    ex_g.finish()
    build(plan, x3_g, [p[1:] for p in ex_g.pieces(wide_g, spread, "future")])
    ex_h.later()
    convolve(plan, x3_g, turned_two, wide_b)
    mean_two, scale_two = moments(reduces[1].finish())

    def unit_two(v):
        return (v - mean_two) * scale_two

    unit = unit_two(wide_h[...])
    lifted = wide_b[...] * slope(unit * gain_two + shift_two) * gain_two
    wide_l[...] = lifted
    reduces[2].start(column_sum(lifted), column_sum(lifted * unit))
    ex_l.start(wide_l, pick)
    reduces[2].middle()
    ex_l.middle(wide_l, spread)
    ex_h.finish()
    build(
        plan,
        x3_two,
        frames_of(
            ex_h.pieces(wide_h, spread, "past"),
            lambda v: silu(unit_two(v) * gain_two + shift_two),
        ),
    )
    ex_l.later()
    kernel_term(plan, x3_two, wide_g[...].T.astype(BF16), acc_two, 0, 9)
    a_two, b_two = group_means(reduces[2].finish())
    advance()
    ex_l.finish()
    frames = []
    for (side, *lifts), (_, *hids) in zip(
        ex_l.pieces(wide_l, spread, "future"), ex_h.pieces(wide_h, spread, "future")
    ):
        out = []
        for border, lift, hid in zip(("up", None, "down"), lifts, hids):
            value = scale_two * (lift - a_two - unit_two(hid) * b_two)
            out.append(jnp.where(valid(plan, place, lift.shape[0], side, border), value, 0.0))
        frames.append(tuple(out))
    build(plan, x3_h, frames)
    advance()
    convolve(plan, x3_h, turned_one, wide_b)
    unit = unit_one(wide_x[...])
    lifted = wide_b[...] * slope(unit * gain_one + shift_one) * gain_one
    reduces[3].start(column_sum(lifted), column_sum(lifted * unit))
    wide_l[...] = lifted
    advance()
    reduces[3].middle()
    w = lax.broadcasted_iota(jnp.int32, (plan.h * plan.wp, c), 0) & (plan.wp - 1)
    own = jnp.concatenate(
        [jnp.where(w < plan.w, frames[f][1], 0.0) for f in range(plan.f)], axis=0
    )
    turned = own.T.astype(BF16)
    ready = min(9, -(-plan.parts[0][1] // (3 * c)))
    kernel_term(plan, x3_one, turned, acc_one, 0, ready)
    steps_one = [item.steps() for item in sums_one]
    steps_one[0].pop(0)()
    advance()
    kernel_term(plan, x3_one, turned, acc_one, ready, 9)
    for steps in steps_one[1:]:
        steps.pop(0)()
    convolve(plan, x3_two, kernel_two, wide_b)
    for steps in steps_one:
        steps.pop(0)()
    advance()
    unspaced(plan, wide_x[...] + wide_b[...], block_out)
    a_one, b_one = group_means(reduces[3].finish())
    unit = unit_one(wide_x[...])
    unspaced(
        plan,
        wide_g[...] + scale_one * (wide_l[...] - a_one - unit * b_one),
        grad_input,
    )
    while steps_one[0]:
        for steps in steps_one:
            steps.pop(0)()
        advance()
    part_two[...] = done_two[pl.ds(0, plan.taps_rows)]
    part_one[...] = done_one[pl.ds(0, plan.taps_rows)]
    for item in exchanges + reduces + sums:
        item.drain()


def block_kernel(plan, features, cotangent, kernel_one, kernel_two, norms):
    c, n = plan.c, plan.n
    half = plan.f * plan.wp
    exchange = []
    n_ex = []
    for count in (1, 1, 2, 1):
        shapes = [(n, c), (2 * plan.cb, c), (2 * plan.cb, c), (2 * half, c), (2 * half, c)]
        shapes += [(n, c), (2 * plan.cb, c), (2 * half, c)] * count
        n_ex.append(len(shapes))
        exchange += [pltpu.VMEM(s, BF16) for s in shapes]
    reduce = [
        pltpu.VMEM((8, c), F32),
        pltpu.VMEM((max(1, plan.na - 1), 8, c), F32),
        pltpu.VMEM((8, c), F32),
        pltpu.VMEM((max(1, plan.nb - 1), 8, c), F32),
    ] * 4
    sems = 4 * EX_SEMS + 4 * (plan.na + plan.nb - 2) + 2 * sum_sems(plan)
    vmem = pl.BlockSpec(memory_space=pltpu.VMEM)
    taps = kernel_one.shape[0]
    return pl.pallas_call(
        functools.partial(body, plan, n_ex),
        out_shape=(
            jax.ShapeDtypeStruct(features.shape, BF16),
            jax.ShapeDtypeStruct(features.shape, BF16),
            jax.ShapeDtypeStruct((taps, c), BF16),
            jax.ShapeDtypeStruct((taps, c), BF16),
        ),
        in_specs=[vmem] * 5,
        out_specs=(vmem,) * 4,
        scratch_shapes=[pltpu.VMEM((n, c), F32)] * 5
        + [pltpu.VMEM((2 * plan.cb, n), BF16), pltpu.VMEM((n, 2 * plan.cb), BF16)]
        + [pltpu.VMEM((taps, c), BF16)] * 2
        + [pltpu.VMEM((plan.np, 3 * c), BF16)] * 4
        + exchange
        + reduce
        + [pltpu.VMEM((plan.sum_rows, c), F32)] * 2
        + [pltpu.VMEM((plan.sum_rows, c), BF16)] * 2
        + sum_scratch(plan)[0] * 2
        + [pltpu.SemaphoreType.DMA((sems,))] * 2,
        compiler_params=pltpu.CompilerParams(
            collective_id=0, has_side_effects=True, vmem_limit_bytes=52 * 2**20
        ),
    )(features, cotangent, kernel_one, kernel_two, norms)


def local(features, cotangent, conv_one, conv_two, gain_one, shift_one, gain_two, shift_two):
    f, h, w, c = features.shape
    plan = Plan(f, h, w, c, tuple(lax.axis_size(a) for a in AXES))
    norms = jnp.stack([gain_one, shift_one, gain_two, shift_two])
    block_out, grad_input, part_one, part_two = block_kernel(
        plan, features, cotangent, conv_one.reshape(-1, c), conv_two.reshape(-1, c), norms
    )
    return (
        block_out,
        grad_input,
        part_one.astype(F32).reshape(conv_one.shape),
        part_two.astype(F32).reshape(conv_two.shape),
    )


def solution(mesh):
    block = P("tm", "row", "col", None)
    return jax.shard_map(
        local,
        mesh=mesh,
        in_specs=(block, block) + (P(),) * 6,
        out_specs=(block, block, P(), P()),
        check_vma=False,
    )
```

```python
import functools

import jax
import jax.numpy as jnp
from jax import lax
from jax.experimental import pallas as pl
from jax.experimental.pallas import tpu as pltpu
from jax.sharding import PartitionSpec as P

GROUPS = 32
EPSILON = 1e-05
MESH = pl.DeviceIdType.MESH
F32 = jnp.float32
BF16 = jnp.bfloat16
AXES = ("tm", "row", "col")


class Plan:
    def __init__(self, f, h, w, c, sizes):
        self.f, self.h, self.w, self.c = f, h, w, c
        self.wp = 16
        while self.wp < w + 2:
            self.wp *= 2
        self.n = f * h * self.wp
        self.hp = h + 2
        self.np = (f + 2) * self.hp * self.wp
        self.cb = -(-(f * h) // 16) * 16
        self.rb = 2 * self.wp
        self.ntm, self.nrow, self.ncol = sizes
        self.na = self.nrow
        self.nb = self.ntm * self.ncol
        self.taps_rows = 27 * c
        unit = 16 * self.ntm * self.nrow * self.ncol
        units = -(-self.taps_rows // unit)
        first = -(-units // 2)
        self.sum_rows = units * unit
        self.parts = [(0, first * unit)]
        if units > first:
            self.parts.append((first * unit, (units - first) * unit))

    def stages(self, order):
        near = 2 if self.ncol % 2 == 0 else 1
        known = dict(
            near=("col", 1, near, True),
            col=("col", near, self.ncol // near, False),
            tm=("tm", 1, self.ntm, False),
            row=("row", 1, self.nrow, True),
        )
        return [known[name] for name in order if known[name][2] > 1]


class Link:
    def __init__(self, src, dst, sems, index, device, sends, receives):
        self.make = lambda: pltpu.make_async_remote_copy(
            src_ref=src,
            dst_ref=dst,
            send_sem=sems[0].at[index],
            recv_sem=sems[1].at[index],
            device_id=device,
            device_id_type=MESH,
        )
        self.sends, self.receives = sends, receives

    def start(self):
        if self.sends is None:
            self.make().start()
            return

        @pl.when(self.sends)
        def _():
            self.make().start()

    def wait_send(self):
        if self.sends is None:
            self.make().wait_send()
            return

        @pl.when(self.sends)
        def _():
            self.make().wait_send()

    def wait_recv(self):
        if self.receives is None:
            self.make().wait_recv()
            return

        @pl.when(self.receives)
        def _():
            self.make().wait_recv()


class Place:
    def __init__(self, plan):
        self.t, self.r, self.c = (lax.axis_index(a) for a in AXES)
        self.has = dict(
            left=self.c > 0,
            right=self.c < plan.ncol - 1,
            up=self.r > 0,
            down=self.r < plan.nrow - 1,
            past=self.t > 0,
            future=self.t < plan.ntm - 1,
        )
        self.dev = dict(
            left={"col": self.c - 1},
            right={"col": self.c + 1},
            up={"row": self.r - 1},
            down={"row": self.r + 1},
            past={"tm": self.t - 1},
            future={"tm": self.t + 1},
        )

    def partners(self, plan):
        rows = [{"row": lax.rem(self.r + d, plan.na)} for d in range(1, plan.na)]
        index = self.t * plan.ncol + self.c
        others = []
        for d in range(1, plan.nb):
            to = lax.rem(index + d, plan.nb)
            others.append({"tm": lax.div(to, plan.ncol), "col": lax.rem(to, plan.ncol)})
        return rows, others


class Reduce:
    def __init__(self, plan, place, refs, sems, base):
        self.own, self.slots_a, self.mid, self.slots_b = refs
        rows, others = place.partners(plan)
        self.a = [
            Link(self.own, self.slots_a.at[d], sems, base + d, dev, None, None)
            for d, dev in enumerate(rows)
        ]
        self.b = [
            Link(self.mid, self.slots_b.at[d], sems, base + len(rows) + d, dev, None, None)
            for d, dev in enumerate(others)
        ]

    def start(self, first, second):
        self.own[...] = jnp.zeros_like(self.own)
        self.own[0:1] = first
        self.own[1:2] = second
        for link in self.a:
            link.start()

    def middle(self):
        for link in self.a:
            link.wait_recv()
        total = self.own[...]
        for d in range(len(self.a)):
            total = total + self.slots_a[d]
        self.mid[...] = total
        for link in self.b:
            link.start()

    def finish(self):
        for link in self.b:
            link.wait_recv()
        total = self.mid[...]
        for d in range(len(self.b)):
            total = total + self.slots_b[d]
        return total

    def drain(self):
        for link in self.a + self.b:
            link.wait_send()


class KernelSum:
    def __init__(self, plan, place, stages, span, acc, done, outs, ins, sems, base):
        self.acc, self.done, self.outs, self.ins = acc, done, outs, ins
        self.stages = stages
        at, count = span
        self.spans, self.reduce, self.gather = [], [], []
        for k, (axis, stride, ways, wide) in enumerate(stages):
            here = dict(tm=place.t, row=place.r, col=place.c)[axis]
            mine = lax.rem(lax.div(here, stride), ways)
            piece = count // ways
            aligned = lambda v: pl.multiple_of(v, 16)
            kept = aligned(at + mine * piece)
            links, sources = [], []
            for d in range(1, ways):
                other = lax.rem(mine + d, ways)
                dev = {axis: here + (other - mine) * stride}
                sent = aligned(at + other * piece)
                if wide:
                    src = acc.at[pl.ds(sent, piece)]
                else:
                    src = outs[k].at[d - 1]
                    sources.append((d - 1, sent))
                links.append((Link(src, ins[k].at[d - 1], sems, base, dev, None, None), dev))
                base += 1
            self.reduce.append([link for link, _ in links])
            gathers = []
            for _, dev in links:
                part = done.at[pl.ds(kept, piece)]
                gathers.append(Link(part, part, sems, base, dev, None, None))
                base += 1
            self.gather.append(gathers)
            self.spans.append((kept, piece, sources))
            at, count = kept, piece
        self.base = base

    def steps(self):
        out = []
        last = len(self.stages) - 1
        for k in range(len(self.stages)):
            out.append(functools.partial(self.reduce_step, k))
        for k in range(last, -1, -1):
            out.append(functools.partial(self.gather_step, k))
        out.append(self.last_step)
        return out

    def reduce_step(self, k):
        if k:
            self.settle(k - 1)
        kept, piece, sources = self.spans[k]
        for slot, sent in sources:
            self.outs[k][slot] = self.acc[pl.ds(sent, piece)].astype(BF16)
        for link in self.reduce[k]:
            link.start()

    def settle(self, k):
        kept, piece, _ = self.spans[k]
        for link in self.reduce[k]:
            link.wait_recv()
        total = self.acc[pl.ds(kept, piece)]
        for d in range(len(self.reduce[k])):
            total = total + self.ins[k][d].astype(F32)
        if k == len(self.stages) - 1:
            self.done[pl.ds(kept, piece)] = total.astype(BF16)
        else:
            self.acc[pl.ds(kept, piece)] = total

    def gather_step(self, k):
        if k == len(self.stages) - 1:
            self.settle(k)
        else:
            for link in self.gather[k + 1]:
                link.wait_recv()
        for link in self.gather[k]:
            link.start()

    def last_step(self):
        for link in self.gather[0]:
            link.wait_recv()

    def drain(self):
        for links in self.reduce + self.gather:
            for link in links:
                link.wait_send()


ORDERS = (("near", "col", "tm", "row"), ("near", "tm", "col", "row"))


def sum_scratch(plan):
    shapes, counts = [], []
    for order, (_, count) in zip(ORDERS, plan.parts):
        outs, ins = [], []
        for axis, stride, ways, wide in plan.stages(order):
            piece = count // ways
            shape = (ways - 1, piece, plan.c)
            outs.append(pltpu.VMEM((1, 16, plan.c) if wide else shape, BF16))
            ins.append(pltpu.VMEM(shape, F32 if wide else BF16))
            count = piece
        counts.append(len(outs))
        shapes += outs + ins
    return shapes, counts


def sum_sems(plan):
    return 2 * sum(
        stage[2] - 1 for order, _ in zip(ORDERS, plan.parts) for stage in plan.stages(order)
    )


EX_SEMS = 10


class Exchange:
    def __init__(self, plan, place, refs, sems, base, directions):
        self.plan, self.place, self.directions = plan, place, directions
        self.own, self.cols_out, self.cols_in, self.rows_out, self.rows_in = refs[:5]
        has, dev = place.has, place.dev
        cb, half = plan.cb, plan.f * plan.wp
        self.cols = [
            Link(self.cols_out.at[pl.ds(0, cb)], self.cols_in.at[pl.ds(0, cb)], sems, base,
                 dev["left"], has["left"], has["right"]),
            Link(self.cols_out.at[pl.ds(cb, cb)], self.cols_in.at[pl.ds(cb, cb)], sems, base + 1,
                 dev["right"], has["right"], has["left"]),
        ]
        self.rows = [
            Link(self.rows_out.at[pl.ds(0, half)], self.rows_in.at[pl.ds(half, half)], sems,
                 base + 2, dev["up"], has["up"], has["down"]),
            Link(self.rows_out.at[pl.ds(half, half)], self.rows_in.at[pl.ds(0, half)], sems,
                 base + 3, dev["down"], has["down"], has["up"]),
        ]
        self.tm = {}
        for k, source in enumerate(directions):
            block, cols, rows = refs[5 + 3 * k : 8 + 3 * k]
            target = "future" if source == "past" else "past"
            links = [
                Link(src, dst, sems, base + 4 + 3 * k + j, dev[target], has[target], has[source])
                for j, (src, dst) in enumerate(
                    [(self.own, block), (self.cols_in, cols), (self.rows_in, rows)]
                )
            ]
            self.tm[source] = ((block, cols, rows), links)

    def clear(self):
        cb, half = self.plan.cb, self.plan.f * self.plan.wp
        has = self.place.has

        def zero(ref, part, cond):
            @pl.when(jnp.logical_not(cond))
            def _():
                ref[part] = jnp.zeros(ref.at[part].shape, ref.dtype)

        zero(self.cols_in, pl.ds(0, cb), has["right"])
        zero(self.cols_in, pl.ds(cb, cb), has["left"])
        zero(self.rows_in, pl.ds(0, half), has["up"])
        zero(self.rows_in, pl.ds(half, half), has["down"])
        for source, (refs, _) in self.tm.items():
            for ref in refs:
                zero(ref, pl.ds(0, ref.shape[0]), has[source])

    def start(self, wide, pick):
        self.own[...] = wide[...].astype(BF16)
        for source in self.directions:
            self.tm[source][1][0].start()
        self.cols_out[...] = jnp.dot(pick[...], self.own[...], preferred_element_type=F32).astype(BF16)
        for link in self.cols:
            link.start()

    def middle(self, wide, spread):
        plan = self.plan
        for link in self.cols:
            link.wait_recv()
        for source in self.directions:
            self.tm[source][1][1].start()
        ends = spread_cols(self.cols_in, spread)
        size = plan.h * plan.wp
        for f in range(plan.f):
            for k, at in enumerate((f * size, (f + 1) * size - plan.wp)):
                self.rows_out[pl.ds((k * plan.f + f) * plan.wp, plan.wp)] = (
                    wide[pl.ds(at, plan.wp)] + ends[at : at + plan.wp]
                ).astype(BF16)
        for link in self.rows:
            link.start()

    def later(self):
        for link in self.rows:
            link.wait_recv()
        for source in self.directions:
            self.tm[source][1][2].start()

    def finish(self):
        for source in self.directions:
            for link in self.tm[source][1]:
                link.wait_recv()

    def drain(self):
        for link in self.cols + self.rows:
            link.wait_send()
        for source in self.directions:
            for link in self.tm[source][1]:
                link.wait_send()

    def pieces(self, wide, spread, source):
        plan = self.plan
        size = plan.h * plan.wp
        (block, cols, rows), _ = self.tm[source]

        def of(value, border, side):
            out = []
            for f in range(plan.f):
                top = border[pl.ds(f * plan.wp, plan.wp)].astype(F32)
                low = border[pl.ds((plan.f + f) * plan.wp, plan.wp)].astype(F32)
                out.append((side, top, value[f * size : (f + 1) * size], low))
            return out

        inner = of(wide[...] + spread_cols(self.cols_in, spread), self.rows_in, None)
        outer = of(block[...].astype(F32) + spread_cols(cols, spread), rows, source)
        if source == "past":
            return outer[plan.f - 2 :] + inner
        return inner + outer[:2]


def spread_cols(cols, spread):
    return jnp.dot(spread[...], cols[...], preferred_element_type=F32)


def silu(v):
    return v / (1.0 + jnp.exp(-v))


def slope(v):
    sigm = 1.0 / (1.0 + jnp.exp(-v))
    return sigm * (1.0 + v * (1.0 - sigm))


def valid(plan, place, count, side, border):
    has = place.has
    w = lax.broadcasted_iota(jnp.int32, (count, plan.c), 0) & (plan.wp - 1)
    one = lambda cond: cond.astype(jnp.int32)
    mask = jnp.where(
        w < plan.w,
        1,
        jnp.where(
            w == plan.w,
            one(has["right"]),
            jnp.where(w == plan.wp - 1, one(has["left"]), 0),
        ),
    )
    for name in (side, border):
        if name is not None:
            mask = mask * one(has[name])
    return mask > 0


def store_shifted(plan, ref, at, value):
    count = value.shape[0]
    rows = value.reshape(count // plan.wp, plan.wp, plan.c)
    before = pltpu.roll(rows, 1, axis=1).reshape(value.shape)
    after = pltpu.roll(rows, plan.wp - 1, axis=1).reshape(value.shape)
    c = plan.c
    ref[pl.ds(at, count), 0:c] = before.astype(BF16)
    ref[pl.ds(at, count), c : 2 * c] = value.astype(BF16)
    ref[pl.ds(at, count), 2 * c : 3 * c] = after.astype(BF16)


def build(plan, ref, frames):
    for k, (top, rows, low) in enumerate(frames):
        at = k * plan.hp * plan.wp
        store_shifted(plan, ref, at, top)
        store_shifted(plan, ref, at + plan.wp, rows)
        store_shifted(plan, ref, at + (plan.h + 1) * plan.wp, low)


def convolve(plan, ref, kernel, out):
    size = plan.h * plan.wp

    def frame(f, carry):
        pieces = []
        for p in range(3):
            for q in range(3):
                at = pl.multiple_of(((f + p) * plan.hp + q) * plan.wp, plan.wp)
                pieces.append(ref[pl.ds(at, size), :])
        wide = jnp.dot(jnp.concatenate(pieces, axis=1), kernel[...], preferred_element_type=F32)
        w = lax.broadcasted_iota(jnp.int32, wide.shape, 0) & (plan.wp - 1)
        out[pl.ds(pl.multiple_of(f * size, size), size), :] = jnp.where(w < plan.w, wide, 0.0)
        return carry

    lax.fori_loop(0, plan.f, frame, 0)


def kernel_term(plan, ref, turned, part, low, high):
    size = plan.h * plan.wp

    def tap(pq, carry):
        p, q = lax.div(pq, 3), lax.rem(pq, 3)
        pieces = []
        for f in range(plan.f):
            at = pl.multiple_of(((f + p) * plan.hp + q) * plan.wp, plan.wp)
            pieces.append(ref[pl.ds(at, size), :])
        term = jnp.dot(turned, jnp.concatenate(pieces, axis=0), preferred_element_type=F32)
        part[pl.ds(pl.multiple_of(pq * 3 * plan.c, 3 * plan.c), 3 * plan.c), :] = term.T
        return carry

    lax.fori_loop(low, high, tap, 0)


def turn_kernel(plan, kernel, out):
    taps, c = 27, plan.c

    def tap(k, carry):
        source = kernel[pl.ds(pl.multiple_of((taps - 1 - k) * c, c), c), :]
        out[pl.ds(pl.multiple_of(k * c, c), c), :] = source.astype(F32).T.astype(BF16)
        return carry

    lax.fori_loop(0, taps, tap, 0)


def spaced(plan, ref, wide):
    wide[...] = jnp.zeros_like(wide)
    for f in range(plan.f):
        for y in range(plan.h):
            wide[pl.ds((f * plan.h + y) * plan.wp, plan.w)] = ref[f, y].astype(F32)


def unspaced(plan, value, ref):
    for f in range(plan.f):
        for y in range(plan.h):
            at = (f * plan.h + y) * plan.wp
            ref[f, y] = value[at : at + plan.w].astype(BF16)


def column_sum(value):
    return jnp.sum(value, axis=0, keepdims=True)


def body(plan, n_ex, *refs):
    refs = list(refs)
    take = lambda k: [refs.pop(0) for _ in range(k)]
    features, cotangent, kernel_one, kernel_two, *norms = take(8)
    block_out, grad_input, part_one, part_two = take(4)
    wide_x, wide_g, wide_h, wide_l, wide_b = take(5)
    pick, spread, turned_one, turned_two = take(4)
    x3_one, x3_two, x3_g, x3_h = take(4)
    exchange_refs = [take(k) for k in n_ex]
    reduce_refs = [take(4) for _ in range(4)]
    acc_one, acc_two, done_one, done_two = take(4)
    sum_refs = []
    for _ in range(2):
        for count in sum_scratch(plan)[1]:
            sum_refs.append((take(count), take(count)))
    sems = take(2)

    place = Place(plan)
    rows, others = place.partners(plan)
    per_reduce = len(rows) + len(others)
    exchanges = [
        Exchange(plan, place, r, sems, EX_SEMS * k, d)
        for k, (r, d) in enumerate(
            zip(exchange_refs, (("past",), ("future",), ("past", "future"), ("future",)))
        )
    ]
    ex_x, ex_g, ex_h, ex_l = exchanges
    reduces = [
        Reduce(plan, place, r, sems, EX_SEMS * 4 + per_reduce * k)
        for k, r in enumerate(reduce_refs)
    ]
    sums = []
    base = EX_SEMS * 4 + per_reduce * 4
    for acc, done in ((acc_two, done_two), (acc_one, done_one)):
        for order, span in zip(ORDERS, plan.parts):
            outs, ins = sum_refs[len(sums)]
            sums.append(
                KernelSum(plan, place, plan.stages(order), span, acc, done, outs, ins, sems, base)
            )
            base = sums[-1].base
        acc[pl.ds(plan.taps_rows, plan.sum_rows - plan.taps_rows)] = jnp.zeros(
            (plan.sum_rows - plan.taps_rows, plan.c), F32
        )
    sums_two, sums_one = sums[: len(plan.parts)], sums[len(plan.parts) :]
    steps_two = [list(group) for group in zip(*[item.steps() for item in sums_two])]

    def advance():
        if steps_two:
            for step in steps_two.pop(0):
                step()

    for ex in exchanges:
        ex.clear()

    barrier = pltpu.get_barrier_semaphore()
    for dev in rows + others:
        pl.semaphore_signal(barrier, inc=1, device_id=dev, device_id_type=MESH)

    c = plan.c
    per_group = c // GROUPS
    members = float(plan.f * plan.h * plan.w * plan.ntm * plan.nrow * plan.ncol * per_group)
    lane_i = lax.broadcasted_iota(jnp.int32, (c, c), 0)
    lane_j = lax.broadcasted_iota(jnp.int32, (c, c), 1)
    same = (lax.div(lane_i, per_group) == lax.div(lane_j, per_group)).astype(F32)

    def group_means(total):
        sums = jnp.dot(
            total, same, preferred_element_type=F32, precision=lax.Precision.HIGHEST
        )
        return sums[0:1] / members, sums[1:2] / members

    def moments(total):
        average, square = group_means(total)
        return average, lax.rsqrt(square - average * average + EPSILON)

    spaced(plan, features, wide_x)
    j = lax.broadcasted_iota(jnp.int32, (2 * plan.cb, plan.n), 0)
    at = lax.broadcasted_iota(jnp.int32, (2 * plan.cb, plan.n), 1)
    first = j < plan.cb
    pick[...] = (
        at == jnp.where(first, j * plan.wp, (j - plan.cb) * plan.wp + plan.w - 1)
    ).astype(F32).astype(BF16)
    at = lax.broadcasted_iota(jnp.int32, (plan.n, 2 * plan.cb), 0)
    j = lax.broadcasted_iota(jnp.int32, (plan.n, 2 * plan.cb), 1)
    first = j < plan.cb
    spread[...] = (
        at == jnp.where(first, j * plan.wp + plan.w, (j - plan.cb) * plan.wp + plan.wp - 1)
    ).astype(F32).astype(BF16)

    turn_kernel(plan, kernel_two, turned_two)
    pl.semaphore_wait(barrier, per_reduce)
    gain_one, shift_one, gain_two, shift_two = (ref[...] for ref in norms)

    x = wide_x[...]
    reduces[0].start(column_sum(x), column_sum(x * x))
    ex_x.start(wide_x, pick)
    spaced(plan, cotangent, wide_g)
    ex_g.start(wide_g, pick)
    reduces[0].middle()
    ex_x.middle(wide_x, spread)
    ex_g.middle(wide_g, spread)
    ex_x.later()
    ex_g.later()
    turn_kernel(plan, kernel_one, turned_one)
    mean_one, scale_one = moments(reduces[0].finish())
    ex_x.finish()

    def unit_one(v):
        return (v - mean_one) * scale_one

    def frames_of(pieces, fn):
        out = []
        for side, top, rows_, low in pieces:
            keep = lambda v, border: jnp.where(
                valid(plan, place, v.shape[0], side, border), fn(v), 0.0
            )
            out.append((keep(top, "up"), keep(rows_, None), keep(low, "down")))
        return out

    build(
        plan,
        x3_one,
        frames_of(
            ex_x.pieces(wide_x, spread, "past"),
            lambda v: silu(unit_one(v) * gain_one + shift_one),
        ),
    )
    convolve(plan, x3_one, kernel_one, wide_h)
    hidden = wide_h[...]
    reduces[1].start(column_sum(hidden), column_sum(hidden * hidden))
    ex_h.start(wide_h, pick)
    reduces[1].middle()
    ex_h.middle(wide_h, spread)
    ex_g.finish()
    build(plan, x3_g, [p[1:] for p in ex_g.pieces(wide_g, spread, "future")])
    ex_h.later()
    convolve(plan, x3_g, turned_two, wide_b)
    mean_two, scale_two = moments(reduces[1].finish())

    def unit_two(v):
        return (v - mean_two) * scale_two

    unit = unit_two(wide_h[...])
    lifted = wide_b[...] * slope(unit * gain_two + shift_two) * gain_two
    wide_l[...] = lifted
    reduces[2].start(column_sum(lifted), column_sum(lifted * unit))
    ex_l.start(wide_l, pick)
    reduces[2].middle()
    ex_l.middle(wide_l, spread)
    ex_h.finish()
    build(
        plan,
        x3_two,
        frames_of(
            ex_h.pieces(wide_h, spread, "past"),
            lambda v: silu(unit_two(v) * gain_two + shift_two),
        ),
    )
    ex_l.later()
    kernel_term(plan, x3_two, wide_g[...].T.astype(BF16), acc_two, 0, 9)
    a_two, b_two = group_means(reduces[2].finish())
    advance()
    ex_l.finish()
    frames = []
    for (side, *lifts), (_, *hids) in zip(
        ex_l.pieces(wide_l, spread, "future"), ex_h.pieces(wide_h, spread, "future")
    ):
        out = []
        for border, lift, hid in zip(("up", None, "down"), lifts, hids):
            value = scale_two * (lift - a_two - unit_two(hid) * b_two)
            out.append(jnp.where(valid(plan, place, lift.shape[0], side, border), value, 0.0))
        frames.append(tuple(out))
    build(plan, x3_h, frames)
    advance()
    w = lax.broadcasted_iota(jnp.int32, (plan.h * plan.wp, c), 0) & (plan.wp - 1)
    own = jnp.concatenate(
        [jnp.where(w < plan.w, frames[f][1], 0.0) for f in range(plan.f)], axis=0
    )
    turned = own.T.astype(BF16)
    ready = min(9, -(-plan.parts[0][1] // (3 * c)))
    kernel_term(plan, x3_one, turned, acc_one, 0, ready)
    steps_one = [item.steps() for item in sums_one]
    steps_one[0].pop(0)()
    advance()
    kernel_term(plan, x3_one, turned, acc_one, ready, 9)
    for steps in steps_one[1:]:
        steps.pop(0)()

    def advance_one():
        for steps in steps_one:
            steps.pop(0)()

    convolve(plan, x3_h, turned_one, wide_b)
    unit = unit_one(wide_x[...])
    lifted = wide_b[...] * slope(unit * gain_one + shift_one) * gain_one
    reduces[3].start(column_sum(lifted), column_sum(lifted * unit))
    wide_l[...] = lifted
    advance_one()
    advance()
    reduces[3].middle()
    convolve(plan, x3_two, kernel_two, wide_b)
    advance_one()
    advance()
    unspaced(plan, wide_x[...] + wide_b[...], block_out)
    a_one, b_one = group_means(reduces[3].finish())
    advance_one()
    advance()
    unit = unit_one(wide_x[...])
    unspaced(
        plan,
        wide_g[...] + scale_one * (wide_l[...] - a_one - unit * b_one),
        grad_input,
    )
    while steps_one[0]:
        advance_one()
        advance()
    part_two[...] = done_two[pl.ds(0, plan.taps_rows)]
    part_one[...] = done_one[pl.ds(0, plan.taps_rows)]
    for item in exchanges + reduces + sums:
        item.drain()


def block_kernel(plan, features, cotangent, kernel_one, kernel_two, *norms):
    c, n = plan.c, plan.n
    half = plan.f * plan.wp
    exchange = []
    n_ex = []
    for count in (1, 1, 2, 1):
        shapes = [(n, c), (2 * plan.cb, c), (2 * plan.cb, c), (2 * half, c), (2 * half, c)]
        shapes += [(n, c), (2 * plan.cb, c), (2 * half, c)] * count
        n_ex.append(len(shapes))
        exchange += [pltpu.VMEM(s, BF16) for s in shapes]
    reduce = [
        pltpu.VMEM((8, c), F32),
        pltpu.VMEM((max(1, plan.na - 1), 8, c), F32),
        pltpu.VMEM((8, c), F32),
        pltpu.VMEM((max(1, plan.nb - 1), 8, c), F32),
    ] * 4
    sems = 4 * EX_SEMS + 4 * (plan.na + plan.nb - 2) + 2 * sum_sems(plan)
    vmem = pl.BlockSpec(memory_space=pltpu.VMEM)
    taps = kernel_one.shape[0]
    return pl.pallas_call(
        functools.partial(body, plan, n_ex),
        out_shape=(
            jax.ShapeDtypeStruct(features.shape, BF16),
            jax.ShapeDtypeStruct(features.shape, BF16),
            jax.ShapeDtypeStruct((taps, c), BF16),
            jax.ShapeDtypeStruct((taps, c), BF16),
        ),
        in_specs=[vmem] * 8,
        out_specs=(vmem,) * 4,
        scratch_shapes=[pltpu.VMEM((n, c), F32)] * 5
        + [pltpu.VMEM((2 * plan.cb, n), BF16), pltpu.VMEM((n, 2 * plan.cb), BF16)]
        + [pltpu.VMEM((taps, c), BF16)] * 2
        + [pltpu.VMEM((plan.np, 3 * c), BF16)] * 4
        + exchange
        + reduce
        + [pltpu.VMEM((plan.sum_rows, c), F32)] * 2
        + [pltpu.VMEM((plan.sum_rows, c), BF16)] * 2
        + sum_scratch(plan)[0] * 2
        + [pltpu.SemaphoreType.DMA((sems,))] * 2,
        compiler_params=pltpu.CompilerParams(
            collective_id=0, has_side_effects=True, vmem_limit_bytes=52 * 2**20
        ),
    )(features, cotangent, kernel_one, kernel_two, *norms)


def local(features, cotangent, conv_one, conv_two, gain_one, shift_one, gain_two, shift_two):
    f, h, w, c = features.shape
    plan = Plan(f, h, w, c, tuple(lax.axis_size(a) for a in AXES))
    norms = [v.reshape(1, c) for v in (gain_one, shift_one, gain_two, shift_two)]
    block_out, grad_input, part_one, part_two = block_kernel(
        plan, features, cotangent, conv_one.reshape(-1, c), conv_two.reshape(-1, c), *norms
    )
    return (
        block_out,
        grad_input,
        part_one.astype(F32).reshape(conv_one.shape),
        part_two.astype(F32).reshape(conv_two.shape),
    )


def solution(mesh):
    block = P("tm", "row", "col", None)
    return jax.shard_map(
        local,
        mesh=mesh,
        in_specs=(block, block) + (P(),) * 6,
        out_specs=(block, block, P(), P()),
        check_vma=False,
    )
```

```python
import functools

import jax
import jax.numpy as jnp
from jax import lax
from jax.experimental import pallas as pl
from jax.experimental.pallas import tpu as pltpu
from jax.sharding import PartitionSpec as P

GROUPS = 32
EPSILON = 1e-05
MESH = pl.DeviceIdType.MESH
F32 = jnp.float32
BF16 = jnp.bfloat16
AXES = ("tm", "row", "col")


class Plan:
    def __init__(self, f, h, w, c, sizes):
        self.f, self.h, self.w, self.c = f, h, w, c
        self.wp = 16
        while self.wp < w + 2:
            self.wp *= 2
        self.n = f * h * self.wp
        self.hp = h + 2
        self.np = (f + 2) * self.hp * self.wp
        self.cb = -(-(f * h) // 16) * 16
        self.rb = 2 * self.wp
        self.ntm, self.nrow, self.ncol = sizes
        self.na = self.nrow
        self.nb = self.ntm * self.ncol
        self.taps_rows = 27 * c
        unit = 16 * self.ntm * self.nrow * self.ncol
        units = -(-self.taps_rows // unit)
        first = -(-units // 2)
        self.sum_rows = units * unit
        self.parts = [(0, first * unit)]
        if units > first:
            self.parts.append((first * unit, (units - first) * unit))

    def stages(self, order):
        near = 2 if self.ncol % 2 == 0 else 1
        known = dict(
            near=("col", 1, near, True),
            col=("col", near, self.ncol // near, False),
            tm=("tm", 1, self.ntm, False),
            row=("row", 1, self.nrow, False),
        )
        return [known[name] for name in order if known[name][2] > 1]


class Link:
    def __init__(self, src, dst, sems, index, device, sends, receives):
        self.make = lambda: pltpu.make_async_remote_copy(
            src_ref=src,
            dst_ref=dst,
            send_sem=sems[0].at[index],
            recv_sem=sems[1].at[index],
            device_id=device,
            device_id_type=MESH,
        )
        self.sends, self.receives = sends, receives

    def start(self):
        if self.sends is None:
            self.make().start()
            return

        @pl.when(self.sends)
        def _():
            self.make().start()

    def wait_send(self):
        if self.sends is None:
            self.make().wait_send()
            return

        @pl.when(self.sends)
        def _():
            self.make().wait_send()

    def wait_recv(self):
        if self.receives is None:
            self.make().wait_recv()
            return

        @pl.when(self.receives)
        def _():
            self.make().wait_recv()


class Place:
    def __init__(self, plan):
        self.t, self.r, self.c = (lax.axis_index(a) for a in AXES)
        self.has = dict(
            left=self.c > 0,
            right=self.c < plan.ncol - 1,
            up=self.r > 0,
            down=self.r < plan.nrow - 1,
            past=self.t > 0,
            future=self.t < plan.ntm - 1,
        )
        self.dev = dict(
            left={"col": self.c - 1},
            right={"col": self.c + 1},
            up={"row": self.r - 1},
            down={"row": self.r + 1},
            past={"tm": self.t - 1},
            future={"tm": self.t + 1},
        )

    def partners(self, plan):
        rows = [{"row": lax.rem(self.r + d, plan.na)} for d in range(1, plan.na)]
        index = self.t * plan.ncol + self.c
        others = []
        for d in range(1, plan.nb):
            to = lax.rem(index + d, plan.nb)
            others.append({"tm": lax.div(to, plan.ncol), "col": lax.rem(to, plan.ncol)})
        return rows, others


class Reduce:
    def __init__(self, plan, place, refs, sems, base):
        self.own, self.slots_a, self.mid, self.slots_b = refs
        rows, others = place.partners(plan)
        self.a = [
            Link(self.own, self.slots_a.at[d], sems, base + d, dev, None, None)
            for d, dev in enumerate(rows)
        ]
        self.b = [
            Link(self.mid, self.slots_b.at[d], sems, base + len(rows) + d, dev, None, None)
            for d, dev in enumerate(others)
        ]

    def start(self, first, second):
        self.own[...] = jnp.zeros_like(self.own)
        self.own[0:1] = first
        self.own[1:2] = second
        for link in self.a:
            link.start()

    def middle(self):
        for link in self.a:
            link.wait_recv()
        total = self.own[...]
        for d in range(len(self.a)):
            total = total + self.slots_a[d]
        self.mid[...] = total
        for link in self.b:
            link.start()

    def finish(self):
        for link in self.b:
            link.wait_recv()
        total = self.mid[...]
        for d in range(len(self.b)):
            total = total + self.slots_b[d]
        return total

    def drain(self):
        for link in self.a + self.b:
            link.wait_send()


class KernelSum:
    def __init__(self, plan, place, stages, span, acc, done, outs, ins, sems, base):
        self.acc, self.done, self.outs, self.ins = acc, done, outs, ins
        self.stages = stages
        at, count = span
        self.spans, self.reduce, self.gather = [], [], []
        for k, (axis, stride, ways, wide) in enumerate(stages):
            here = dict(tm=place.t, row=place.r, col=place.c)[axis]
            mine = lax.rem(lax.div(here, stride), ways)
            piece = count // ways
            aligned = lambda v: pl.multiple_of(v, 16)
            kept = aligned(at + mine * piece)
            links, sources = [], []
            for d in range(1, ways):
                other = lax.rem(mine + d, ways)
                dev = {axis: here + (other - mine) * stride}
                sent = aligned(at + other * piece)
                if wide:
                    src = acc.at[pl.ds(sent, piece)]
                else:
                    src = outs[k].at[d - 1]
                    sources.append((d - 1, sent))
                links.append((Link(src, ins[k].at[d - 1], sems, base, dev, None, None), dev))
                base += 1
            self.reduce.append([link for link, _ in links])
            gathers = []
            for _, dev in links:
                part = done.at[pl.ds(kept, piece)]
                gathers.append(Link(part, part, sems, base, dev, None, None))
                base += 1
            self.gather.append(gathers)
            self.spans.append((kept, piece, sources))
            at, count = kept, piece
        self.base = base

    def steps(self):
        out = []
        last = len(self.stages) - 1
        for k in range(len(self.stages)):
            out.append(functools.partial(self.reduce_step, k))
        for k in range(last, -1, -1):
            out.append(functools.partial(self.gather_step, k))
        out.append(self.last_step)
        return out

    def reduce_step(self, k):
        if k:
            self.settle(k - 1)
        kept, piece, sources = self.spans[k]
        for slot, sent in sources:
            self.outs[k][slot] = self.acc[pl.ds(sent, piece)].astype(BF16)
        for link in self.reduce[k]:
            link.start()

    def settle(self, k):
        kept, piece, _ = self.spans[k]
        for link in self.reduce[k]:
            link.wait_recv()
        total = self.acc[pl.ds(kept, piece)]
        for d in range(len(self.reduce[k])):
            total = total + self.ins[k][d].astype(F32)
        if k == len(self.stages) - 1:
            self.done[pl.ds(kept, piece)] = total.astype(BF16)
        else:
            self.acc[pl.ds(kept, piece)] = total

    def gather_step(self, k):
        if k == len(self.stages) - 1:
            self.settle(k)
        else:
            for link in self.gather[k + 1]:
                link.wait_recv()
        for link in self.gather[k]:
            link.start()

    def last_step(self):
        for link in self.gather[0]:
            link.wait_recv()

    def drain(self):
        for links in self.reduce + self.gather:
            for link in links:
                link.wait_send()


ORDERS = (("near", "col", "tm", "row"), ("near", "tm", "col", "row"))


def sum_scratch(plan):
    shapes, counts = [], []
    for order, (_, count) in zip(ORDERS, plan.parts):
        outs, ins = [], []
        for axis, stride, ways, wide in plan.stages(order):
            piece = count // ways
            shape = (ways - 1, piece, plan.c)
            outs.append(pltpu.VMEM((1, 16, plan.c) if wide else shape, BF16))
            ins.append(pltpu.VMEM(shape, F32 if wide else BF16))
            count = piece
        counts.append(len(outs))
        shapes += outs + ins
    return shapes, counts


def sum_sems(plan):
    return 2 * sum(
        stage[2] - 1 for order, _ in zip(ORDERS, plan.parts) for stage in plan.stages(order)
    )


EX_SEMS = 10


class Exchange:
    def __init__(self, plan, place, refs, sems, base, directions):
        self.plan, self.place, self.directions = plan, place, directions
        self.own, self.cols_out, self.cols_in, self.rows_out, self.rows_in = refs[:5]
        has, dev = place.has, place.dev
        cb, half = plan.cb, plan.f * plan.wp
        self.cols = [
            Link(self.cols_out.at[pl.ds(0, cb)], self.cols_in.at[pl.ds(0, cb)], sems, base,
                 dev["left"], has["left"], has["right"]),
            Link(self.cols_out.at[pl.ds(cb, cb)], self.cols_in.at[pl.ds(cb, cb)], sems, base + 1,
                 dev["right"], has["right"], has["left"]),
        ]
        self.rows = [
            Link(self.rows_out.at[pl.ds(0, half)], self.rows_in.at[pl.ds(half, half)], sems,
                 base + 2, dev["up"], has["up"], has["down"]),
            Link(self.rows_out.at[pl.ds(half, half)], self.rows_in.at[pl.ds(0, half)], sems,
                 base + 3, dev["down"], has["down"], has["up"]),
        ]
        self.tm = {}
        for k, source in enumerate(directions):
            block, cols, rows = refs[5 + 3 * k : 8 + 3 * k]
            target = "future" if source == "past" else "past"
            links = [
                Link(src, dst, sems, base + 4 + 3 * k + j, dev[target], has[target], has[source])
                for j, (src, dst) in enumerate(
                    [(self.own, block), (self.cols_in, cols), (self.rows_in, rows)]
                )
            ]
            self.tm[source] = ((block, cols, rows), links)

    def clear(self):
        cb, half = self.plan.cb, self.plan.f * self.plan.wp
        has = self.place.has

        def zero(ref, part, cond):
            @pl.when(jnp.logical_not(cond))
            def _():
                ref[part] = jnp.zeros(ref.at[part].shape, ref.dtype)

        zero(self.cols_in, pl.ds(0, cb), has["right"])
        zero(self.cols_in, pl.ds(cb, cb), has["left"])
        zero(self.rows_in, pl.ds(0, half), has["up"])
        zero(self.rows_in, pl.ds(half, half), has["down"])
        for source, (refs, _) in self.tm.items():
            for ref in refs:
                zero(ref, pl.ds(0, ref.shape[0]), has[source])

    def start(self, wide, pick):
        self.own[...] = wide[...].astype(BF16)
        for source in self.directions:
            self.tm[source][1][0].start()
        self.cols_out[...] = jnp.dot(pick[...], self.own[...], preferred_element_type=F32).astype(BF16)
        for link in self.cols:
            link.start()

    def middle(self, wide, spread):
        plan = self.plan
        for link in self.cols:
            link.wait_recv()
        for source in self.directions:
            self.tm[source][1][1].start()
        ends = spread_cols(self.cols_in, spread)
        size = plan.h * plan.wp
        for f in range(plan.f):
            for k, at in enumerate((f * size, (f + 1) * size - plan.wp)):
                self.rows_out[pl.ds((k * plan.f + f) * plan.wp, plan.wp)] = (
                    wide[pl.ds(at, plan.wp)] + ends[at : at + plan.wp]
                ).astype(BF16)
        for link in self.rows:
            link.start()

    def later(self):
        for link in self.rows:
            link.wait_recv()
        for source in self.directions:
            self.tm[source][1][2].start()

    def finish(self):
        for source in self.directions:
            for link in self.tm[source][1]:
                link.wait_recv()

    def drain(self):
        for link in self.cols + self.rows:
            link.wait_send()
        for source in self.directions:
            for link in self.tm[source][1]:
                link.wait_send()

    def pieces(self, wide, spread, source):
        plan = self.plan
        size = plan.h * plan.wp
        (block, cols, rows), _ = self.tm[source]

        def of(value, border, side):
            out = []
            for f in range(plan.f):
                top = border[pl.ds(f * plan.wp, plan.wp)].astype(F32)
                low = border[pl.ds((plan.f + f) * plan.wp, plan.wp)].astype(F32)
                out.append((side, top, value[f * size : (f + 1) * size], low))
            return out

        inner = of(wide[...] + spread_cols(self.cols_in, spread), self.rows_in, None)
        outer = of(block[...].astype(F32) + spread_cols(cols, spread), rows, source)
        if source == "past":
            return outer[plan.f - 2 :] + inner
        return inner + outer[:2]


def spread_cols(cols, spread):
    return jnp.dot(spread[...], cols[...], preferred_element_type=F32)


def silu(v):
    return v / (1.0 + jnp.exp(-v))


def slope(v):
    sigm = 1.0 / (1.0 + jnp.exp(-v))
    return sigm * (1.0 + v * (1.0 - sigm))


def valid(plan, place, count, side, border):
    has = place.has
    w = lax.broadcasted_iota(jnp.int32, (count, plan.c), 0) & (plan.wp - 1)
    one = lambda cond: cond.astype(jnp.int32)
    mask = jnp.where(
        w < plan.w,
        1,
        jnp.where(
            w == plan.w,
            one(has["right"]),
            jnp.where(w == plan.wp - 1, one(has["left"]), 0),
        ),
    )
    for name in (side, border):
        if name is not None:
            mask = mask * one(has[name])
    return mask > 0


def store_shifted(plan, ref, at, value):
    count = value.shape[0]
    rows = value.reshape(count // plan.wp, plan.wp, plan.c)
    before = pltpu.roll(rows, 1, axis=1).reshape(value.shape)
    after = pltpu.roll(rows, plan.wp - 1, axis=1).reshape(value.shape)
    c = plan.c
    ref[pl.ds(at, count), 0:c] = before.astype(BF16)
    ref[pl.ds(at, count), c : 2 * c] = value.astype(BF16)
    ref[pl.ds(at, count), 2 * c : 3 * c] = after.astype(BF16)


def build(plan, ref, frames):
    for k, (top, rows, low) in enumerate(frames):
        at = k * plan.hp * plan.wp
        store_shifted(plan, ref, at, top)
        store_shifted(plan, ref, at + plan.wp, rows)
        store_shifted(plan, ref, at + (plan.h + 1) * plan.wp, low)


def convolve(plan, ref, kernel, out):
    size = plan.h * plan.wp

    def frame(f, carry):
        pieces = []
        for p in range(3):
            for q in range(3):
                at = pl.multiple_of(((f + p) * plan.hp + q) * plan.wp, plan.wp)
                pieces.append(ref[pl.ds(at, size), :])
        wide = jnp.dot(jnp.concatenate(pieces, axis=1), kernel[...], preferred_element_type=F32)
        w = lax.broadcasted_iota(jnp.int32, wide.shape, 0) & (plan.wp - 1)
        out[pl.ds(pl.multiple_of(f * size, size), size), :] = jnp.where(w < plan.w, wide, 0.0)
        return carry

    lax.fori_loop(0, plan.f, frame, 0)


def kernel_term(plan, ref, turned, part, low, high):
    size = plan.h * plan.wp

    def tap(pq, carry):
        p, q = lax.div(pq, 3), lax.rem(pq, 3)
        pieces = []
        for f in range(plan.f):
            at = pl.multiple_of(((f + p) * plan.hp + q) * plan.wp, plan.wp)
            pieces.append(ref[pl.ds(at, size), :])
        term = jnp.dot(turned, jnp.concatenate(pieces, axis=0), preferred_element_type=F32)
        part[pl.ds(pl.multiple_of(pq * 3 * plan.c, 3 * plan.c), 3 * plan.c), :] = term.T
        return carry

    lax.fori_loop(low, high, tap, 0)


def turn_kernel(plan, kernel, out):
    taps, c = 27, plan.c

    def tap(k, carry):
        source = kernel[pl.ds(pl.multiple_of((taps - 1 - k) * c, c), c), :]
        out[pl.ds(pl.multiple_of(k * c, c), c), :] = source.astype(F32).T.astype(BF16)
        return carry

    lax.fori_loop(0, taps, tap, 0)


def spaced(plan, ref, wide):
    wide[...] = jnp.zeros_like(wide)
    for f in range(plan.f):
        for y in range(plan.h):
            wide[pl.ds((f * plan.h + y) * plan.wp, plan.w)] = ref[f, y].astype(F32)


def unspaced(plan, value, ref):
    for f in range(plan.f):
        for y in range(plan.h):
            at = (f * plan.h + y) * plan.wp
            ref[f, y] = value[at : at + plan.w].astype(BF16)


def column_sum(value):
    return jnp.sum(value, axis=0, keepdims=True)


def body(plan, n_ex, *refs):
    refs = list(refs)
    take = lambda k: [refs.pop(0) for _ in range(k)]
    features, cotangent, kernel_one, kernel_two, *norms = take(8)
    block_out, grad_input, part_one, part_two = take(4)
    wide_x, wide_g, wide_h, wide_l, wide_b = take(5)
    pick, spread, turned_one, turned_two = take(4)
    x3_one, x3_two, x3_g, x3_h = take(4)
    exchange_refs = [take(k) for k in n_ex]
    reduce_refs = [take(4) for _ in range(4)]
    acc_one, acc_two, done_one, done_two = take(4)
    sum_refs = []
    for _ in range(2):
        for count in sum_scratch(plan)[1]:
            sum_refs.append((take(count), take(count)))
    sems = take(2)

    place = Place(plan)
    rows, others = place.partners(plan)
    per_reduce = len(rows) + len(others)
    exchanges = [
        Exchange(plan, place, r, sems, EX_SEMS * k, d)
        for k, (r, d) in enumerate(
            zip(exchange_refs, (("past",), ("future",), ("past", "future"), ("future",)))
        )
    ]
    ex_x, ex_g, ex_h, ex_l = exchanges
    reduces = [
        Reduce(plan, place, r, sems, EX_SEMS * 4 + per_reduce * k)
        for k, r in enumerate(reduce_refs)
    ]
    sums = []
    base = EX_SEMS * 4 + per_reduce * 4
    for acc, done in ((acc_two, done_two), (acc_one, done_one)):
        for order, span in zip(ORDERS, plan.parts):
            outs, ins = sum_refs[len(sums)]
            sums.append(
                KernelSum(plan, place, plan.stages(order), span, acc, done, outs, ins, sems, base)
            )
            base = sums[-1].base
        acc[pl.ds(plan.taps_rows, plan.sum_rows - plan.taps_rows)] = jnp.zeros(
            (plan.sum_rows - plan.taps_rows, plan.c), F32
        )
    sums_two, sums_one = sums[: len(plan.parts)], sums[len(plan.parts) :]
    steps_two = [list(group) for group in zip(*[item.steps() for item in sums_two])]

    def advance():
        if steps_two:
            for step in steps_two.pop(0):
                step()

    for ex in exchanges:
        ex.clear()

    barrier = pltpu.get_barrier_semaphore()
    for dev in rows + others:
        pl.semaphore_signal(barrier, inc=1, device_id=dev, device_id_type=MESH)

    c = plan.c
    per_group = c // GROUPS
    members = float(plan.f * plan.h * plan.w * plan.ntm * plan.nrow * plan.ncol * per_group)
    lane_i = lax.broadcasted_iota(jnp.int32, (c, c), 0)
    lane_j = lax.broadcasted_iota(jnp.int32, (c, c), 1)
    same = (lax.div(lane_i, per_group) == lax.div(lane_j, per_group)).astype(F32)

    def group_means(total):
        sums = jnp.dot(
            total, same, preferred_element_type=F32, precision=lax.Precision.HIGHEST
        )
        return sums[0:1] / members, sums[1:2] / members

    def moments(total):
        average, square = group_means(total)
        return average, lax.rsqrt(square - average * average + EPSILON)

    spaced(plan, features, wide_x)
    j = lax.broadcasted_iota(jnp.int32, (2 * plan.cb, plan.n), 0)
    at = lax.broadcasted_iota(jnp.int32, (2 * plan.cb, plan.n), 1)
    first = j < plan.cb
    pick[...] = (
        at == jnp.where(first, j * plan.wp, (j - plan.cb) * plan.wp + plan.w - 1)
    ).astype(F32).astype(BF16)
    at = lax.broadcasted_iota(jnp.int32, (plan.n, 2 * plan.cb), 0)
    j = lax.broadcasted_iota(jnp.int32, (plan.n, 2 * plan.cb), 1)
    first = j < plan.cb
    spread[...] = (
        at == jnp.where(first, j * plan.wp + plan.w, (j - plan.cb) * plan.wp + plan.wp - 1)
    ).astype(F32).astype(BF16)

    pl.semaphore_wait(barrier, per_reduce)
    gain_one, shift_one, gain_two, shift_two = (ref[...] for ref in norms)

    x = wide_x[...]
    reduces[0].start(column_sum(x), column_sum(x * x))
    ex_x.start(wide_x, pick)
    spaced(plan, cotangent, wide_g)
    ex_g.start(wide_g, pick)
    reduces[0].middle()
    ex_x.middle(wide_x, spread)
    ex_g.middle(wide_g, spread)
    turn_kernel(plan, kernel_two, turned_two)
    ex_x.later()
    ex_g.later()
    turn_kernel(plan, kernel_one, turned_one)
    mean_one, scale_one = moments(reduces[0].finish())
    ex_x.finish()

    def unit_one(v):
        return (v - mean_one) * scale_one

    def frames_of(pieces, fn):
        out = []
        for side, top, rows_, low in pieces:
            keep = lambda v, border: jnp.where(
                valid(plan, place, v.shape[0], side, border), fn(v), 0.0
            )
            out.append((keep(top, "up"), keep(rows_, None), keep(low, "down")))
        return out

    build(
        plan,
        x3_one,
        frames_of(
            ex_x.pieces(wide_x, spread, "past"),
            lambda v: silu(unit_one(v) * gain_one + shift_one),
        ),
    )
    convolve(plan, x3_one, kernel_one, wide_h)
    hidden = wide_h[...]
    reduces[1].start(column_sum(hidden), column_sum(hidden * hidden))
    ex_h.start(wide_h, pick)
    reduces[1].middle()
    ex_h.middle(wide_h, spread)
    ex_g.finish()
    build(plan, x3_g, [p[1:] for p in ex_g.pieces(wide_g, spread, "future")])
    ex_h.later()
    convolve(plan, x3_g, turned_two, wide_b)
    mean_two, scale_two = moments(reduces[1].finish())

    def unit_two(v):
        return (v - mean_two) * scale_two

    unit = unit_two(wide_h[...])
    lifted = wide_b[...] * slope(unit * gain_two + shift_two) * gain_two
    wide_l[...] = lifted
    reduces[2].start(column_sum(lifted), column_sum(lifted * unit))
    ex_l.start(wide_l, pick)
    reduces[2].middle()
    ex_l.middle(wide_l, spread)
    ex_h.finish()
    build(
        plan,
        x3_two,
        frames_of(
            ex_h.pieces(wide_h, spread, "past"),
            lambda v: silu(unit_two(v) * gain_two + shift_two),
        ),
    )
    ex_l.later()
    kernel_term(plan, x3_two, wide_g[...].T.astype(BF16), acc_two, 0, 9)
    a_two, b_two = group_means(reduces[2].finish())
    advance()
    ex_l.finish()
    frames = []
    for (side, *lifts), (_, *hids) in zip(
        ex_l.pieces(wide_l, spread, "future"), ex_h.pieces(wide_h, spread, "future")
    ):
        out = []
        for border, lift, hid in zip(("up", None, "down"), lifts, hids):
            value = scale_two * (lift - a_two - unit_two(hid) * b_two)
            out.append(jnp.where(valid(plan, place, lift.shape[0], side, border), value, 0.0))
        frames.append(tuple(out))
    build(plan, x3_h, frames)
    advance()
    w = lax.broadcasted_iota(jnp.int32, (plan.h * plan.wp, c), 0) & (plan.wp - 1)
    own = jnp.concatenate(
        [jnp.where(w < plan.w, frames[f][1], 0.0) for f in range(plan.f)], axis=0
    )
    turned = own.T.astype(BF16)
    ready = min(9, -(-plan.parts[0][1] // (3 * c)))
    kernel_term(plan, x3_one, turned, acc_one, 0, ready)
    steps_one = [item.steps() for item in sums_one]
    steps_one[0].pop(0)()
    advance()
    kernel_term(plan, x3_one, turned, acc_one, ready, 9)
    for steps in steps_one[1:]:
        steps.pop(0)()

    def advance_one():
        for steps in steps_one:
            steps.pop(0)()

    convolve(plan, x3_h, turned_one, wide_b)
    unit = unit_one(wide_x[...])
    lifted = wide_b[...] * slope(unit * gain_one + shift_one) * gain_one
    reduces[3].start(column_sum(lifted), column_sum(lifted * unit))
    wide_l[...] = lifted
    advance_one()
    advance()
    reduces[3].middle()
    convolve(plan, x3_two, kernel_two, wide_b)
    advance_one()
    advance()
    unspaced(plan, wide_x[...] + wide_b[...], block_out)
    a_one, b_one = group_means(reduces[3].finish())
    advance_one()
    advance()
    unit = unit_one(wide_x[...])
    unspaced(
        plan,
        wide_g[...] + scale_one * (wide_l[...] - a_one - unit * b_one),
        grad_input,
    )
    while steps_one[0]:
        advance_one()
        advance()
    part_two[...] = done_two[pl.ds(0, plan.taps_rows)]
    part_one[...] = done_one[pl.ds(0, plan.taps_rows)]
    for item in exchanges + reduces + sums:
        item.drain()


def block_kernel(plan, features, cotangent, kernel_one, kernel_two, *norms):
    c, n = plan.c, plan.n
    half = plan.f * plan.wp
    exchange = []
    n_ex = []
    for count in (1, 1, 2, 1):
        shapes = [(n, c), (2 * plan.cb, c), (2 * plan.cb, c), (2 * half, c), (2 * half, c)]
        shapes += [(n, c), (2 * plan.cb, c), (2 * half, c)] * count
        n_ex.append(len(shapes))
        exchange += [pltpu.VMEM(s, BF16) for s in shapes]
    reduce = [
        pltpu.VMEM((8, c), F32),
        pltpu.VMEM((max(1, plan.na - 1), 8, c), F32),
        pltpu.VMEM((8, c), F32),
        pltpu.VMEM((max(1, plan.nb - 1), 8, c), F32),
    ] * 4
    sems = 4 * EX_SEMS + 4 * (plan.na + plan.nb - 2) + 2 * sum_sems(plan)
    vmem = pl.BlockSpec(memory_space=pltpu.VMEM)
    taps = kernel_one.shape[0]
    return pl.pallas_call(
        functools.partial(body, plan, n_ex),
        out_shape=(
            jax.ShapeDtypeStruct(features.shape, BF16),
            jax.ShapeDtypeStruct(features.shape, BF16),
            jax.ShapeDtypeStruct((taps, c), BF16),
            jax.ShapeDtypeStruct((taps, c), BF16),
        ),
        in_specs=[vmem] * 8,
        out_specs=(vmem,) * 4,
        scratch_shapes=[pltpu.VMEM((n, c), F32)] * 5
        + [pltpu.VMEM((2 * plan.cb, n), BF16), pltpu.VMEM((n, 2 * plan.cb), BF16)]
        + [pltpu.VMEM((taps, c), BF16)] * 2
        + [pltpu.VMEM((plan.np, 3 * c), BF16)] * 4
        + exchange
        + reduce
        + [pltpu.VMEM((plan.sum_rows, c), F32)] * 2
        + [pltpu.VMEM((plan.sum_rows, c), BF16)] * 2
        + sum_scratch(plan)[0] * 2
        + [pltpu.SemaphoreType.DMA((sems,))] * 2,
        compiler_params=pltpu.CompilerParams(
            collective_id=0, has_side_effects=True, vmem_limit_bytes=52 * 2**20
        ),
    )(features, cotangent, kernel_one, kernel_two, *norms)


def local(features, cotangent, conv_one, conv_two, gain_one, shift_one, gain_two, shift_two):
    f, h, w, c = features.shape
    plan = Plan(f, h, w, c, tuple(lax.axis_size(a) for a in AXES))
    norms = [v.reshape(1, c) for v in (gain_one, shift_one, gain_two, shift_two)]
    block_out, grad_input, part_one, part_two = block_kernel(
        plan, features, cotangent, conv_one.reshape(-1, c), conv_two.reshape(-1, c), *norms
    )
    return (
        block_out,
        grad_input,
        part_one.astype(F32).reshape(conv_one.shape),
        part_two.astype(F32).reshape(conv_two.shape),
    )


def solution(mesh):
    block = P("tm", "row", "col", None)
    return jax.shard_map(
        local,
        mesh=mesh,
        in_specs=(block, block) + (P(),) * 6,
        out_specs=(block, block, P(), P()),
        check_vma=False,
    )
```
